128 devices in a mesh: occi: 8 (over y, z_lo), occj: 16 (over x, z_hi, core).
Axes of the slice: x: 4, y: 4, z: 4 (z_hi: 2, z_lo: 2; z = z_hi * 2 + z_lo), core: 2. Of those that a mesh axis runs over, the one named last changes fastest.
Arguments:
- amplitudes: bfloat16 [16, 16, 512, 512], P('occi', 'occj'), may hold values from -6 to 6
- exch_int: bfloat16 [16, 16, 512, 512], P('occi', 'occj'), may hold values from -6 to 6
- thc_factor: bfloat16 [512, 2048], replicated, may hold values from -0.25 to 0.25
- thc_core: bfloat16 [2048, 2048], replicated, may hold values from -1.5 to 1.5
- fock_vir: bfloat16 [512, 512], replicated, may hold values from -0.25 to 0.25
- eps_vir: float32 [512], replicated, may hold values from 0.5 to 3
- eps_occ: float32 [16], replicated, may hold values from -1.5 to -0.2
- fock_occ: float32 [16, 16], replicated, may hold values from -1.8 to 1.8
- couple_list: int32 [16, 6], replicated, may hold values from 0 to 15, as said below
- couple_count: int32 [16], replicated, may hold values from 1 to 6, as said below
Outputs:
- residual: float32 [16, 16, 512, 512], P('occi', 'occj')
- amplitudes_new: bfloat16 [16, 16, 512, 512], P('occi', 'occj')
The draws below stay inside these ranges and needn't reach their ends.
Inputs may be any that keep to these rules, and one draw needn't show every extreme that they name: `couple_list`: row j holds 6 distinct orbitals, none of them j. `couple_count`: some row uses all 6 entries.
All inputs are finite; a program needn't handle non-finite values.
Results may differ from the reference program's by a relative error of at most 0.0045.
Values may be sent and summed in bfloat16 or wider, within the bound.
No kernel may reach another device: no remote copies, remote signals or barrier semaphores. Data moves between devices by JAX's collectives and lax.ppermute only.
A program may use at most 128 MiB of HBM per device.

```python
import math
import jax
import jax.numpy as jnp
from jax import lax

V = 512
RANK = 2048
LMAX = 6
NO = 16


def draw_couple_list(key, part):
    scores = jax.random.randint(jax.random.fold_in(key, 11), (NO, NO), 0, 2 ** 20)
    ranked = scores * NO + jnp.arange(NO, dtype=jnp.int32)[None, :]
    ranked = jnp.where(jnp.eye(NO, dtype=bool), 2 ** 30, ranked)
    ordering = jnp.argsort(ranked, axis=1, stable=True)
    return ordering[:, :LMAX].astype(jnp.int32)


def draw_couple_count(key, part):
    counts = jax.random.randint(jax.random.fold_in(key, 23), (NO,), 1, LMAX + 1)
    heaviest = jax.random.randint(jax.random.fold_in(key, 29), (), 0, NO)
    return jnp.where(jnp.arange(NO) == heaviest, LMAX, counts).astype(jnp.int32)


def block_scale(key, extent, split, least, largest):
    def one(axis_at, shards_of):
        steps = jax.random.uniform(jax.random.fold_in(jax.random.fold_in(key, 6), axis_at), (shards_of,), jnp.float32, least / len(split), largest / len(split))
        return jnp.repeat(jnp.exp(steps), extent[axis_at] // shards_of).reshape((-1,) + (1,) * (len(extent) - axis_at - 1))

    factor_of = one(*split[0])
    for cut in split[1:]:
        factor_of = factor_of * one(*cut)
    return factor_of


def normal_values(rng, shape, deviation, bound, shards=(), kind=jnp.bfloat16):
    drawn = jax.random.normal(rng, shape, jnp.float32) * deviation
    if len(shards) > 0:
        drawn = block_scale(rng, shape, shards, -0.22, 0.18) * drawn
    return jnp.clip(drawn, min=-bound, max=bound).astype(kind)


def setup_inputs(seed: int = 0) -> dict:
    seeds = jax.random.split(jax.random.key(seed), 11)
    return {
        "amplitudes": normal_values(seeds[0], (NO, NO, V, V), 1.0, 6.0, ((0, 8), (1, 16))),
        "exch_int": normal_values(seeds[1], (NO, NO, V, V), 1.0, 6.0, ((0, 8), (1, 16))),
        "thc_factor": normal_values(seeds[2], (V, RANK), V ** -0.5, 0.25),
        "thc_core": normal_values(seeds[3], (RANK, RANK), 0.25, 1.5),
        "fock_vir": normal_values(seeds[4], (V, V), V ** -0.5, 0.25),
        "eps_vir": jnp.clip(jnp.exp(jax.random.uniform(seeds[5], (V,), jnp.float32, math.log(0.5), math.log(3.0))), 0.5, 3.0),
        "eps_occ": jnp.clip(jax.random.uniform(seeds[6], (NO,), jnp.float32, -1.5, -0.2), -1.5, -0.2),
        "fock_occ": normal_values(seeds[7], (NO, NO), 0.3, 1.8, (), jnp.float32),
        "couple_list": draw_couple_list(jax.random.fold_in(seeds[10], 71), 0),
        "couple_count": draw_couple_count(jax.random.fold_in(seeds[10], 71), 0),
    }


def coupling(fock_occ, couple_list, couple_count):
    n_occ = fock_occ.shape[0]
    slots = jnp.arange(couple_list.shape[1], dtype=jnp.int32)
    active = slots[None, :] < couple_count[:, None]
    target = jnp.arange(n_occ, dtype=jnp.int32)
    hits = (couple_list[:, :, None] == target[None, None, :]) & active[:, :, None]
    return fock_occ * jnp.sum(hits.astype(fock_occ.dtype), axis=1)


def pair_terms(amp_pair, integral, thc_factor, thc_core, fock_vir):
    first = jnp.dot(amp_pair, thc_factor, preferred_element_type=jnp.float32).astype(jnp.bfloat16)
    middle = lax.dot_general(thc_factor, first, (((0,), (0,)), ((), ())), preferred_element_type=jnp.float32)
    scaled = (thc_core.astype(jnp.float32) * middle).astype(jnp.bfloat16)
    second = jnp.dot(thc_factor, scaled, preferred_element_type=jnp.float32).astype(jnp.bfloat16)
    ladder = lax.dot_general(second, thc_factor, (((1,), (1,)), ((), ())), preferred_element_type=jnp.float32)
    virtual = jnp.dot(fock_vir, amp_pair, preferred_element_type=jnp.float32)
    return integral.astype(jnp.float32) + ladder + virtual


def reference(amplitudes, exch_int, thc_factor, thc_core, fock_vir, eps_vir, eps_occ, fock_occ, couple_list, couple_count):
    n_occ = amplitudes.shape[0]
    virt = amplitudes.shape[2]
    weights = coupling(fock_occ, couple_list, couple_count)
    flat_amps = amplitudes.reshape(n_occ * n_occ, virt, virt)
    flat_ints = exch_int.reshape(n_occ * n_occ, virt, virt)
    local_terms = lax.map(lambda pair_in: pair_terms(pair_in[0], pair_in[1], thc_factor, thc_core, fock_vir), (flat_amps, flat_ints))
    local_terms = local_terms.reshape(n_occ, n_occ, virt, virt)

    def occupied_row(row_amps):
        return -jnp.einsum('jk,kab->jab', weights, row_amps.astype(jnp.float32), precision=lax.Precision.HIGHEST)

    occupied = lax.map(occupied_row, amplitudes)
    half = local_terms + occupied
    residual = half + jnp.transpose(half, (1, 0, 3, 2))
    denominator = eps_vir[None, None, :, None] + eps_vir[None, None, None, :] - eps_occ[:, None, None, None] - eps_occ[None, :, None, None]
    updated = (amplitudes.astype(jnp.float32) - residual / denominator).astype(jnp.bfloat16)
    return residual, updated
```

```python
import functools

import jax
import jax.numpy as jnp
from jax import lax
from jax.experimental import pallas as pl
from jax.experimental.pallas import tpu as pltpu
from jax.sharding import PartitionSpec as P

AXES = ("occi", "occj")
F32 = jnp.float32
BF16 = jnp.bfloat16
SUB = 16


def coupling(fock_occ, couple_list, couple_count):
    n_occ = fock_occ.shape[0]
    slots = jnp.arange(couple_list.shape[1], dtype=jnp.int32)
    active = slots[None, :] < couple_count[:, None]
    target = jnp.arange(n_occ, dtype=jnp.int32)
    hits = (couple_list[:, :, None] == target[None, None, :]) & active[:, :, None]
    return fock_occ * jnp.sum(hits.astype(fock_occ.dtype), axis=1)


def params(limit, **kw):
    return pltpu.CompilerParams(vmem_limit_bytes=limit << 20, **kw)


def whole(shape):
    return pl.BlockSpec(shape, lambda *_: (0,) * len(shape))


def pack_kernel(n, place, amp_ref, *outs):
    core, chip = place[0], place[1]
    block = outs[0].shape[0]
    for e in range(n):
        rows = pl.ds(pl.multiple_of((chip ^ (e >> 1)) * block, block), block)
        outs[e][...] = amp_ref[core ^ (e & 1), rows, :]


def pack(place, amps, n):
    _, virt, _ = amps.shape
    block = virt * 2 // n
    return pl.pallas_call(
        functools.partial(pack_kernel, n),
        out_shape=[jax.ShapeDtypeStruct((block, virt), BF16)] * n,
        grid_spec=pltpu.PrefetchScalarGridSpec(
            num_scalar_prefetch=1,
            grid=(1,),
            in_specs=[whole(amps.shape)],
            out_specs=[whole((block, virt))] * n,
        ),
        compiler_params=params(16),
        cost_estimate=pl.CostEstimate(flops=0, bytes_accessed=4 * amps.size, transcendentals=0),
        name="pack",
    )(place, amps)


def mix_kernel(n, w_ref, *refs):
    ins, outs = refs[:n], refs[n:]
    block = ins[0].shape[0]
    w = w_ref[...]
    high = w.astype(BF16)
    rest = w - high.astype(F32)
    mid = rest.astype(BF16)
    low = (rest - mid.astype(F32)).astype(BF16)
    for r in range(0, block, SUB):
        rhs = jnp.concatenate([ref[r : r + SUB, :] for ref in ins], axis=0)
        total = jnp.dot(high, rhs, preferred_element_type=F32)
        total += jnp.dot(mid, rhs, preferred_element_type=F32)
        total += jnp.dot(low, rhs, preferred_element_type=F32)
        for e in range(n):
            outs[e][r : r + SUB, :] = total[e * SUB : (e + 1) * SUB, :].astype(BF16)


def mix(wide, slices):
    n = len(slices)
    shape = slices[0].shape
    return pl.pallas_call(
        functools.partial(mix_kernel, n),
        out_shape=[jax.ShapeDtypeStruct(shape, BF16)] * n,
        grid=(1,),
        in_specs=[whole(wide.shape)] + [whole(shape)] * n,
        out_specs=[whole(shape)] * n,
        compiler_params=params(24),
        cost_estimate=pl.CostEstimate(
            flops=10**9, bytes_accessed=4 * n * shape[0] * shape[1], transcendentals=0
        ),
        name="mix",
    )(wide, *slices)


def ladder_kernel(slot, amp_ref, int_ref, x_ref, xt_ref, core_ref, fock_ref, out_ref, scaled):
    step = pl.program_id(0)
    tile = core_ref.shape[1]
    rank = x_ref.shape[1]
    chunk = min(512, rank)
    amp = amp_ref[...]
    cols = pl.ds(pl.multiple_of(step * tile, tile), tile)
    first = jnp.dot(amp, x_ref[:, cols], preferred_element_type=F32).astype(BF16)
    for p in range(0, rank, chunk):
        middle = jnp.dot(xt_ref[p : p + chunk, :], first, preferred_element_type=F32)
        scaled[p : p + chunk, :] = (core_ref[p : p + chunk, :].astype(F32) * middle).astype(BF16)
    second = jnp.dot(x_ref[...], scaled[...], preferred_element_type=F32).astype(BF16)
    part = jnp.dot(second, xt_ref[cols, :], preferred_element_type=F32)

    @pl.when(step == 0)
    def _():
        virtual = jnp.dot(fock_ref[...], amp, preferred_element_type=F32)
        out_ref[...] = int_ref[...].astype(F32) + virtual + part

    @pl.when(step > 0)
    def _():
        out_ref[...] += part


def ladder(slot, amps, ints, x, xt, core, fock):
    virt, rank = x.shape
    tile = min(512, rank)
    pair = pl.BlockSpec((None, virt, virt), lambda q, s: (s[0], 0, 0))
    return pl.pallas_call(
        ladder_kernel,
        out_shape=jax.ShapeDtypeStruct((virt, virt), F32),
        grid_spec=pltpu.PrefetchScalarGridSpec(
            num_scalar_prefetch=1,
            grid=(rank // tile,),
            in_specs=[
                pair,
                pair,
                whole(x.shape),
                whole(xt.shape),
                pl.BlockSpec((rank, tile), lambda q, s: (0, q)),
                whole(fock.shape),
            ],
            out_specs=whole((virt, virt)),
            scratch_shapes=[pltpu.VMEM((rank, tile), BF16)],
        ),
        compiler_params=params(40, dimension_semantics=("arbitrary",)),
        cost_estimate=pl.CostEstimate(
            flops=4 * virt * rank * (rank + virt) + 2 * virt**3,
            bytes_accessed=2 * rank * rank + 4 * virt * rank,
            transcendentals=0,
        ),
        name="ladder",
    )(slot, amps, ints, x, xt, core, fock)


def half_kernel(n, place, part_ref, *refs):
    slices, (half_ref, send_ref) = refs[:n], refs[n:]
    block = slices[0].shape[0]
    chip = place[1]
    for d in range(n):
        rows = pl.ds(pl.multiple_of((chip ^ d) * block, block), block)
        half = part_ref[rows, :] - slices[d][...].astype(F32)
        half_ref[rows, :] = half
        send_ref[rows, :] = half.astype(BF16)


def half_of(place, part, slices):
    n = len(slices)
    shape = part.shape
    return pl.pallas_call(
        functools.partial(half_kernel, n),
        out_shape=[jax.ShapeDtypeStruct(shape, F32), jax.ShapeDtypeStruct(shape, BF16)],
        grid_spec=pltpu.PrefetchScalarGridSpec(
            num_scalar_prefetch=1,
            grid=(1,),
            in_specs=[whole(shape)] + [whole(slices[0].shape)] * n,
            out_specs=[whole(shape)] * 2,
        ),
        compiler_params=params(16),
        cost_estimate=pl.CostEstimate(flops=0, bytes_accessed=12 * part.size, transcendentals=0),
        name="half",
    )(place, part, *slices)


def finish_kernel(slot, half_ref, mirror_ref, amp_ref, col_ref, row_ref, occ_ref, *refs):
    res_ref, new_ref = refs[-2:]
    residual = half_ref[...] + mirror_ref[...].astype(F32).T
    denominator = col_ref[...] + row_ref[...] - occ_ref[0] - occ_ref[1]
    res_ref[...] = residual
    new_ref[...] = (amp_ref[...].astype(F32) - residual / denominator).astype(BF16)


def finish(slot, half, mirror, amps, eps_col, eps_row, occ, held):
    virt = half.shape[0]
    rows = min(128, virt)
    strip = pl.BlockSpec((None, rows, virt), lambda r, s: (s[0], r, 0))
    held_specs = [pl.BlockSpec(memory_space=pl.ANY)] * len(held)
    return pl.pallas_call(
        finish_kernel,
        out_shape=[
            jax.ShapeDtypeStruct(amps.shape, F32),
            jax.ShapeDtypeStruct(amps.shape, BF16),
        ],
        grid_spec=pltpu.PrefetchScalarGridSpec(
            num_scalar_prefetch=1,
            grid=(virt // rows,),
            in_specs=[
                pl.BlockSpec((rows, virt), lambda r, s: (r, 0)),
                pl.BlockSpec((virt, rows), lambda r, s: (0, r)),
                strip,
                pl.BlockSpec((rows, 1), lambda r, s: (r, 0)),
                whole((1, virt)),
                pl.BlockSpec(memory_space=pltpu.SMEM),
            ]
            + held_specs,
            out_specs=[strip, strip],
        ),
        input_output_aliases={7 + n: n for n in range(len(held))},
        compiler_params=params(16, dimension_semantics=("arbitrary",)),
        cost_estimate=pl.CostEstimate(
            flops=20 * half.size, bytes_accessed=14 * half.size, transcendentals=0
        ),
        name="finish",
    )(slot, half, mirror, amps, eps_col, eps_row, occ, *held)


def shards(
    amplitudes,
    exch_int,
    thc_factor,
    thc_core,
    fock_vir,
    eps_vir,
    eps_occ,
    fock_occ,
    couple_list,
    couple_count,
):
    rows_i, _, virt, _ = amplitudes.shape
    n_first = lax.axis_size("occi")
    n_second = lax.axis_size("occj")
    me_i = lax.axis_index("occi")
    me_j = lax.axis_index("occj")
    core = me_j % 2
    place = jnp.stack([core, me_j // 2]).astype(jnp.int32)
    slot_a = jnp.reshape(core, (1,)).astype(jnp.int32)
    slot_b = 1 - slot_a
    amps = amplitudes.reshape(rows_i, virt, virt)
    ints = exch_int.reshape(rows_i, virt, virt)

    def row_hop(e):
        return [
            (p * n_second + m, p * n_second + (m ^ e))
            for p in range(n_first)
            for m in range(n_second)
        ]

    def mirror_hop(flip):
        return [
            (p * n_second + 2 * q + s, q * n_second + 2 * p + (s ^ flip))
            for p in range(n_first)
            for q in range(n_first)
            for s in range(2)
        ]

    weights = coupling(fock_occ, couple_list, couple_count)
    ids = jnp.arange(n_second, dtype=jnp.int32)
    pick = (ids ^ me_j)[:, None] == ids[None, :]
    weights = jnp.sum(jnp.where(pick[:, :, None], weights[None], 0.0), axis=1)
    weights = jnp.sum(jnp.where(pick[None], weights[:, None, :], 0.0), axis=2)
    tall = jnp.repeat(jnp.repeat(weights, SUB, axis=0), SUB, axis=1)
    lane = jnp.arange(n_second * SUB, dtype=jnp.int32) % SUB
    wide = jnp.where(lane[:, None] == lane[None, :], tall, 0.0)

    slices = pack(place, amps, n_second)
    slices = [slices[0]] + [lax.ppermute(slices[e], AXES, row_hop(e)) for e in range(1, n_second)]
    factor_t = thc_factor.T
    part_a = ladder(slot_a, amps, ints, thc_factor, factor_t, thc_core, fock_vir)
    sums = mix(wide, slices)
    sums = [sums[0]] + [lax.ppermute(sums[e], AXES, row_hop(e)) for e in range(1, n_second)]
    part_b = ladder(slot_b, amps, ints, thc_factor, factor_t, thc_core, fock_vir)
    half_a, send_a = half_of(place, part_a, sums[0::2])
    half_b, send_b = half_of(place, part_b, sums[1::2])
    got_a = lax.ppermute(send_a, AXES, mirror_hop(0))
    got_b = lax.ppermute(send_b, AXES, mirror_hop(1))

    occ_rows = lax.dynamic_slice_in_dim(eps_occ, me_i * rows_i, rows_i, 0)
    occ_column = lax.dynamic_slice_in_dim(eps_occ, me_j, 1, 0)
    occ_a = jnp.stack([jnp.where(core == 0, occ_rows[0], occ_rows[1]), occ_column[0]])
    occ_b = jnp.stack([jnp.where(core == 0, occ_rows[1], occ_rows[0]), occ_column[0]])
    eps_col = eps_vir.reshape(virt, 1)
    eps_row = eps_vir.reshape(1, virt)
    held = finish(slot_a, half_a, got_a, amps, eps_col, eps_row, occ_a, ())
    residual, updated = finish(slot_b, half_b, got_b, amps, eps_col, eps_row, occ_b, held)
    return (
        residual.reshape(rows_i, 1, virt, virt),
        updated.reshape(rows_i, 1, virt, virt),
    )


def solution(mesh):
    pairs = P("occi", "occj", None, None)
    return jax.shard_map(
        shards,
        mesh=mesh,
        in_specs=(pairs, pairs) + (P(),) * 8,
        out_specs=(pairs, pairs),
        check_vma=False,
    )
```

```python
import functools

import jax
import jax.numpy as jnp
from jax import lax
from jax.experimental import pallas as pl
from jax.experimental.pallas import tpu as pltpu
from jax.sharding import PartitionSpec as P

AXES = ("occi", "occj")
F32 = jnp.float32
BF16 = jnp.bfloat16
SUB = 16


def coupling(fock_occ, couple_list, couple_count):
    n_occ = fock_occ.shape[0]
    slots = jnp.arange(couple_list.shape[1], dtype=jnp.int32)
    active = slots[None, :] < couple_count[:, None]
    target = jnp.arange(n_occ, dtype=jnp.int32)
    hits = (couple_list[:, :, None] == target[None, None, :]) & active[:, :, None]
    return fock_occ * jnp.sum(hits.astype(fock_occ.dtype), axis=1)


def params(limit, **kw):
    return pltpu.CompilerParams(vmem_limit_bytes=limit << 20, **kw)


def whole(shape):
    return pl.BlockSpec(shape, lambda *_: (0,) * len(shape))


def mix_kernel(w_ref, in_ref, out_ref):
    n, block, _ = in_ref.shape
    w = w_ref[...]
    high = w.astype(BF16)
    rest = w - high.astype(F32)
    mid = rest.astype(BF16)
    low = (rest - mid.astype(F32)).astype(BF16)
    for r in range(0, block, SUB):
        rhs = jnp.concatenate([in_ref[k, r : r + SUB, :] for k in range(n)], axis=0)
        total = jnp.dot(high, rhs, preferred_element_type=F32)
        total += jnp.dot(mid, rhs, preferred_element_type=F32)
        total += jnp.dot(low, rhs, preferred_element_type=F32)
        for j in range(n):
            out_ref[j, r : r + SUB, :] = total[j * SUB : (j + 1) * SUB, :].astype(BF16)


def mix(wide, slices):
    return pl.pallas_call(
        mix_kernel,
        out_shape=jax.ShapeDtypeStruct(slices.shape, BF16),
        grid=(1,),
        in_specs=[whole(wide.shape), whole(slices.shape)],
        out_specs=whole(slices.shape),
        compiler_params=params(24),
        cost_estimate=pl.CostEstimate(
            flops=10**9, bytes_accessed=4 * slices.size, transcendentals=0
        ),
        name="mix",
    )(wide, slices)


def ladder_kernel(slot, amp_ref, int_ref, x_ref, xt_ref, core_ref, fock_ref, out_ref, scaled):
    step = pl.program_id(0)
    tile = core_ref.shape[1]
    rank = x_ref.shape[1]
    chunk = min(512, rank)
    amp = amp_ref[...]
    cols = pl.ds(pl.multiple_of(step * tile, tile), tile)
    first = jnp.dot(amp, x_ref[:, cols], preferred_element_type=F32).astype(BF16)
    for p in range(0, rank, chunk):
        middle = jnp.dot(xt_ref[p : p + chunk, :], first, preferred_element_type=F32)
        scaled[p : p + chunk, :] = (core_ref[p : p + chunk, :].astype(F32) * middle).astype(BF16)
    second = jnp.dot(x_ref[...], scaled[...], preferred_element_type=F32).astype(BF16)
    part = jnp.dot(second, xt_ref[cols, :], preferred_element_type=F32)

    @pl.when(step == 0)
    def _():
        virtual = jnp.dot(fock_ref[...], amp, preferred_element_type=F32)
        out_ref[...] = int_ref[...].astype(F32) + virtual + part

    @pl.when(step > 0)
    def _():
        out_ref[...] += part


def ladder(slot, amps, ints, x, xt, core, fock):
    virt, rank = x.shape
    tile = min(512, rank)
    pair = pl.BlockSpec((None, virt, virt), lambda q, s: (s[0], 0, 0))
    return pl.pallas_call(
        ladder_kernel,
        out_shape=jax.ShapeDtypeStruct((virt, virt), F32),
        grid_spec=pltpu.PrefetchScalarGridSpec(
            num_scalar_prefetch=1,
            grid=(rank // tile,),
            in_specs=[
                pair,
                pair,
                whole(x.shape),
                whole(xt.shape),
                pl.BlockSpec((rank, tile), lambda q, s: (0, q)),
                whole(fock.shape),
            ],
            out_specs=whole((virt, virt)),
            scratch_shapes=[pltpu.VMEM((rank, tile), BF16)],
        ),
        compiler_params=params(40, dimension_semantics=("arbitrary",)),
        cost_estimate=pl.CostEstimate(
            flops=4 * virt * rank * (rank + virt) + 2 * virt**3,
            bytes_accessed=2 * rank * rank + 4 * virt * rank,
            transcendentals=0,
        ),
        name="ladder",
    )(slot, amps, ints, x, xt, core, fock)


def half_kernel(place, part_a, part_b, sum_ref, send_a, send_b):
    core = place[0]
    send_a[...] = (part_a[...] - sum_ref[core].astype(F32)).astype(BF16)
    send_b[...] = (part_b[...] - sum_ref[1 - core].astype(F32)).astype(BF16)


def half_of(place, part_a, part_b, sums):
    virt = part_a.shape[0]
    rows = min(128, virt)
    strip = pl.BlockSpec((rows, virt), lambda r, s: (r, 0))
    return pl.pallas_call(
        half_kernel,
        out_shape=[jax.ShapeDtypeStruct(part_a.shape, BF16)] * 2,
        grid_spec=pltpu.PrefetchScalarGridSpec(
            num_scalar_prefetch=1,
            grid=(virt // rows,),
            in_specs=[strip, strip, pl.BlockSpec((2, rows, virt), lambda r, s: (0, r, 0))],
            out_specs=[strip, strip],
        ),
        compiler_params=params(16),
        cost_estimate=pl.CostEstimate(
            flops=0, bytes_accessed=16 * part_a.size, transcendentals=0
        ),
        name="half",
    )(place, part_a, part_b, sums)


def finish_kernel(slot, part_ref, sum_ref, mirror_ref, amp_ref, col_ref, row_ref, occ_ref, *refs):
    res_ref, new_ref = refs[-2:]
    half = part_ref[...] - sum_ref[...].astype(F32)
    residual = half + mirror_ref[...].astype(F32).T
    denominator = col_ref[...] + row_ref[...] - occ_ref[0] - occ_ref[1]
    res_ref[...] = residual
    new_ref[...] = (amp_ref[...].astype(F32) - residual / denominator).astype(BF16)


def finish(slot, part, sums, mirror, amps, eps_col, eps_row, occ, held):
    virt = part.shape[0]
    rows = min(128, virt)
    strip = pl.BlockSpec((None, rows, virt), lambda r, s: (s[0], r, 0))
    held_specs = [pl.BlockSpec(memory_space=pl.ANY)] * len(held)
    return pl.pallas_call(
        finish_kernel,
        out_shape=[
            jax.ShapeDtypeStruct(amps.shape, F32),
            jax.ShapeDtypeStruct(amps.shape, BF16),
        ],
        grid_spec=pltpu.PrefetchScalarGridSpec(
            num_scalar_prefetch=1,
            grid=(virt // rows,),
            in_specs=[
                pl.BlockSpec((rows, virt), lambda r, s: (r, 0)),
                strip,
                pl.BlockSpec((virt, rows), lambda r, s: (0, r)),
                strip,
                pl.BlockSpec((rows, 1), lambda r, s: (r, 0)),
                whole((1, virt)),
                pl.BlockSpec(memory_space=pltpu.SMEM),
            ]
            + held_specs,
            out_specs=[strip, strip],
        ),
        input_output_aliases={8 + n: n for n in range(len(held))},
        compiler_params=params(16, dimension_semantics=("arbitrary",)),
        cost_estimate=pl.CostEstimate(
            flops=20 * part.size, bytes_accessed=14 * part.size, transcendentals=0
        ),
        name="finish",
    )(slot, part, sums, mirror, amps, eps_col, eps_row, occ, *held)


def shards(
    amplitudes,
    exch_int,
    thc_factor,
    thc_core,
    fock_vir,
    eps_vir,
    eps_occ,
    fock_occ,
    couple_list,
    couple_count,
):
    rows_i, _, virt, _ = amplitudes.shape
    n_first = lax.axis_size("occi")
    n_second = lax.axis_size("occj")
    me_i = lax.axis_index("occi")
    me_j = lax.axis_index("occj")
    core = me_j % 2
    place = jnp.stack([core, me_j // 2]).astype(jnp.int32)
    slot_a = jnp.reshape(core, (1,)).astype(jnp.int32)
    slot_b = 1 - slot_a
    amps = amplitudes.reshape(rows_i, virt, virt)
    ints = exch_int.reshape(rows_i, virt, virt)

    def mirror_hop(flip):
        return [
            (p * n_second + 2 * q + s, q * n_second + 2 * p + (s ^ flip))
            for p in range(n_first)
            for q in range(n_first)
            for s in range(2)
        ]

    slices = amps.reshape(n_second, rows_i * virt // n_second, virt)
    slices = lax.all_to_all(slices, "occj", 0, 0, tiled=True)
    weights = coupling(fock_occ, couple_list, couple_count)
    tall = jnp.repeat(jnp.repeat(weights, SUB, axis=0), SUB, axis=1)
    lane = jnp.arange(n_second * SUB, dtype=jnp.int32) % SUB
    wide = jnp.where(lane[:, None] == lane[None, :], tall, 0.0)
    factor_t = thc_factor.T
    part_a = ladder(slot_a, amps, ints, thc_factor, factor_t, thc_core, fock_vir)
    slices, part_a = lax.optimization_barrier((slices, part_a))
    sums = mix(wide, slices)
    sums = lax.all_to_all(sums, "occj", 0, 0, tiled=True)
    part_b = ladder(slot_b, amps, ints, thc_factor, factor_t, thc_core, fock_vir)
    sums, part_b = lax.optimization_barrier((sums, part_b))
    sums = sums.reshape(rows_i, virt, virt)
    send_a, send_b = half_of(place, part_a, part_b, sums)
    got_a = lax.ppermute(send_a, AXES, mirror_hop(0))
    got_b = lax.ppermute(send_b, AXES, mirror_hop(1))

    occ_rows = lax.dynamic_slice_in_dim(eps_occ, me_i * rows_i, rows_i, 0)
    occ_column = lax.dynamic_slice_in_dim(eps_occ, me_j, 1, 0)
    occ_a = jnp.stack([jnp.where(core == 0, occ_rows[0], occ_rows[1]), occ_column[0]])
    occ_b = jnp.stack([jnp.where(core == 0, occ_rows[1], occ_rows[0]), occ_column[0]])
    eps_col = eps_vir.reshape(virt, 1)
    eps_row = eps_vir.reshape(1, virt)
    held = finish(slot_a, part_a, sums, got_a, amps, eps_col, eps_row, occ_a, ())
    residual, updated = finish(slot_b, part_b, sums, got_b, amps, eps_col, eps_row, occ_b, held)
    return (
        residual.reshape(rows_i, 1, virt, virt),
        updated.reshape(rows_i, 1, virt, virt),
    )


def solution(mesh):
    pairs = P("occi", "occj", None, None)
    return jax.shard_map(
        shards,
        mesh=mesh,
        in_specs=(pairs, pairs) + (P(),) * 8,
        out_specs=(pairs, pairs),
        check_vma=False,
    )
```

```python
import functools

import jax
import jax.numpy as jnp
from jax import lax
from jax.experimental import pallas as pl
from jax.experimental.pallas import tpu as pltpu
from jax.sharding import PartitionSpec as P

AXES = ("occi", "occj")
F32 = jnp.float32
BF16 = jnp.bfloat16
SUB = 16


def coupling(fock_occ, couple_list, couple_count):
    n_occ = fock_occ.shape[0]
    slots = jnp.arange(couple_list.shape[1], dtype=jnp.int32)
    active = slots[None, :] < couple_count[:, None]
    target = jnp.arange(n_occ, dtype=jnp.int32)
    hits = (couple_list[:, :, None] == target[None, None, :]) & active[:, :, None]
    return fock_occ * jnp.sum(hits.astype(fock_occ.dtype), axis=1)


def params(limit, **kw):
    return pltpu.CompilerParams(vmem_limit_bytes=limit << 20, **kw)


def whole(shape):
    return pl.BlockSpec(shape, lambda *_: (0,) * len(shape))


def mix_kernel(w_ref, in_ref, out_ref):
    n = in_ref.shape[0]
    w = w_ref[...]
    high = w.astype(BF16)
    rest = w - high.astype(F32)
    mid = rest.astype(BF16)
    low = (rest - mid.astype(F32)).astype(BF16)
    rhs = jnp.concatenate([in_ref[k] for k in range(n)], axis=0)
    total = jnp.dot(high, rhs, preferred_element_type=F32)
    total += jnp.dot(mid, rhs, preferred_element_type=F32)
    total += jnp.dot(low, rhs, preferred_element_type=F32)
    for j in range(n):
        out_ref[j] = total[j * SUB : (j + 1) * SUB, :].astype(BF16)


def mix(wide, slices):
    n, block, virt = slices.shape
    strip = pl.BlockSpec((n, SUB, virt), lambda r: (0, r, 0))
    return pl.pallas_call(
        mix_kernel,
        out_shape=jax.ShapeDtypeStruct(slices.shape, BF16),
        grid=(block // SUB,),
        in_specs=[whole(wide.shape), strip],
        out_specs=strip,
        compiler_params=params(16),
        cost_estimate=pl.CostEstimate(
            flops=10**9, bytes_accessed=4 * slices.size, transcendentals=0
        ),
        name="mix",
    )(wide, slices)


def ladder_kernel(slot, amp_ref, int_ref, x_ref, core_ref, fock_ref, out_ref, scaled, x_t):
    step = pl.program_id(0)
    tile = core_ref.shape[1]
    rank = x_ref.shape[1]
    chunk = min(512, rank)
    amp = amp_ref[...]

    @pl.when(step == 0)
    def _():
        for c in range(0, rank, min(256, rank)):
            cut = slice(c, c + min(256, rank))
            x_t[cut, :] = x_ref[:, cut].T
        virtual = jnp.dot(fock_ref[...], amp, preferred_element_type=F32)
        out_ref[...] = int_ref[...].astype(F32) + virtual

    cols = pl.ds(pl.multiple_of(step * tile, tile), tile)
    first = jnp.dot(amp, x_ref[:, cols], preferred_element_type=F32).astype(BF16)
    for p in range(0, rank, chunk):
        middle = jnp.dot(x_t[p : p + chunk, :], first, preferred_element_type=F32)
        scaled[p : p + chunk, :] = (core_ref[p : p + chunk, :].astype(F32) * middle).astype(BF16)
    second = jnp.dot(x_ref[...], scaled[...], preferred_element_type=F32).astype(BF16)
    out_ref[...] += jnp.dot(second, x_t[cols, :], preferred_element_type=F32)


def ladder(slot, amps, ints, x, core, fock):
    virt, rank = x.shape
    tile = min(512, rank)
    pair = pl.BlockSpec((None, virt, virt), lambda q, s: (s[0], 0, 0))
    return pl.pallas_call(
        ladder_kernel,
        out_shape=jax.ShapeDtypeStruct((virt, virt), F32),
        grid_spec=pltpu.PrefetchScalarGridSpec(
            num_scalar_prefetch=1,
            grid=(rank // tile,),
            in_specs=[
                pair,
                pair,
                whole(x.shape),
                pl.BlockSpec((rank, tile), lambda q, s: (0, q)),
                whole(fock.shape),
            ],
            out_specs=whole((virt, virt)),
            scratch_shapes=[pltpu.VMEM((rank, tile), BF16), pltpu.VMEM((rank, virt), BF16)],
        ),
        compiler_params=params(56, dimension_semantics=("arbitrary",)),
        cost_estimate=pl.CostEstimate(
            flops=4 * virt * rank * (rank + virt) + 2 * virt**3,
            bytes_accessed=2 * rank * rank + 4 * virt * rank,
            transcendentals=0,
        ),
        name="ladder",
    )(slot, amps, ints, x, core, fock)


def half_kernel(place, part_a, part_b, sum_ref, send_a, send_b):
    core = place[0]
    send_a[...] = (part_a[...] - sum_ref[core].astype(F32)).astype(BF16)
    send_b[...] = (part_b[...] - sum_ref[1 - core].astype(F32)).astype(BF16)


def half_of(place, part_a, part_b, sums):
    virt = part_a.shape[0]
    rows = min(128, virt)
    strip = pl.BlockSpec((rows, virt), lambda r, s: (r, 0))
    return pl.pallas_call(
        half_kernel,
        out_shape=[jax.ShapeDtypeStruct(part_a.shape, BF16)] * 2,
        grid_spec=pltpu.PrefetchScalarGridSpec(
            num_scalar_prefetch=1,
            grid=(virt // rows,),
            in_specs=[strip, strip, pl.BlockSpec((2, rows, virt), lambda r, s: (0, r, 0))],
            out_specs=[strip, strip],
        ),
        compiler_params=params(16),
        cost_estimate=pl.CostEstimate(
            flops=0, bytes_accessed=16 * part_a.size, transcendentals=0
        ),
        name="half",
    )(place, part_a, part_b, sums)


def finish_kernel(slot, part_ref, sum_ref, mirror_ref, amp_ref, col_ref, row_ref, occ_ref, *refs):
    res_ref, new_ref = refs[-2:]
    half = part_ref[...] - sum_ref[...].astype(F32)
    residual = half + mirror_ref[...].astype(F32).T
    denominator = col_ref[...] + row_ref[...] - occ_ref[0] - occ_ref[1]
    res_ref[...] = residual
    new_ref[...] = (amp_ref[...].astype(F32) - residual / denominator).astype(BF16)


def finish(slot, part, sums, mirror, amps, eps_col, eps_row, occ, held):
    virt = part.shape[0]
    rows = min(128, virt)
    strip = pl.BlockSpec((None, rows, virt), lambda r, s: (s[0], r, 0))
    held_specs = [pl.BlockSpec(memory_space=pl.ANY)] * len(held)
    return pl.pallas_call(
        finish_kernel,
        out_shape=[
            jax.ShapeDtypeStruct(amps.shape, F32),
            jax.ShapeDtypeStruct(amps.shape, BF16),
        ],
        grid_spec=pltpu.PrefetchScalarGridSpec(
            num_scalar_prefetch=1,
            grid=(virt // rows,),
            in_specs=[
                pl.BlockSpec((rows, virt), lambda r, s: (r, 0)),
                strip,
                pl.BlockSpec((virt, rows), lambda r, s: (0, r)),
                strip,
                pl.BlockSpec((rows, 1), lambda r, s: (r, 0)),
                whole((1, virt)),
                pl.BlockSpec(memory_space=pltpu.SMEM),
            ]
            + held_specs,
            out_specs=[strip, strip],
        ),
        input_output_aliases={8 + n: n for n in range(len(held))},
        compiler_params=params(16, dimension_semantics=("arbitrary",)),
        cost_estimate=pl.CostEstimate(
            flops=20 * part.size, bytes_accessed=14 * part.size, transcendentals=0
        ),
        name="finish",
    )(slot, part, sums, mirror, amps, eps_col, eps_row, occ, *held)


def shards(
    amplitudes,
    exch_int,
    thc_factor,
    thc_core,
    fock_vir,
    eps_vir,
    eps_occ,
    fock_occ,
    couple_list,
    couple_count,
):
    rows_i, _, virt, _ = amplitudes.shape
    n_first = lax.axis_size("occi")
    n_second = lax.axis_size("occj")
    me_i = lax.axis_index("occi")
    me_j = lax.axis_index("occj")
    core = me_j % 2
    place = jnp.stack([core, me_j // 2]).astype(jnp.int32)
    slot_a = jnp.reshape(core, (1,)).astype(jnp.int32)
    slot_b = 1 - slot_a
    amps = amplitudes.reshape(rows_i, virt, virt)
    ints = exch_int.reshape(rows_i, virt, virt)

    def mirror_hop(flip):
        return [
            (p * n_second + 2 * q + s, q * n_second + 2 * p + (s ^ flip))
            for p in range(n_first)
            for q in range(n_first)
            for s in range(2)
        ]

    slices = amps.reshape(n_second, rows_i * virt // n_second, virt)
    slices = lax.all_to_all(slices, "occj", 0, 0, tiled=True)
    weights = coupling(fock_occ, couple_list, couple_count)
    tall = jnp.repeat(jnp.repeat(weights, SUB, axis=0), SUB, axis=1)
    lane = jnp.arange(n_second * SUB, dtype=jnp.int32) % SUB
    wide = jnp.where(lane[:, None] == lane[None, :], tall, 0.0)
    part_a = ladder(slot_a, amps, ints, thc_factor, thc_core, fock_vir)
    slices, part_a = lax.optimization_barrier((slices, part_a))
    sums = mix(wide, slices)
    sums = lax.all_to_all(sums, "occj", 0, 0, tiled=True)
    part_b = ladder(slot_b, amps, ints, thc_factor, thc_core, fock_vir)
    sums, part_b = lax.optimization_barrier((sums, part_b))
    sums = sums.reshape(rows_i, virt, virt)
    send_a, send_b = half_of(place, part_a, part_b, sums)
    got_a = lax.ppermute(send_a, AXES, mirror_hop(0))
    got_b = lax.ppermute(send_b, AXES, mirror_hop(1))

    occ_rows = lax.dynamic_slice_in_dim(eps_occ, me_i * rows_i, rows_i, 0)
    occ_column = lax.dynamic_slice_in_dim(eps_occ, me_j, 1, 0)
    occ_a = jnp.stack([jnp.where(core == 0, occ_rows[0], occ_rows[1]), occ_column[0]])
    occ_b = jnp.stack([jnp.where(core == 0, occ_rows[1], occ_rows[0]), occ_column[0]])
    eps_col = eps_vir.reshape(virt, 1)
    eps_row = eps_vir.reshape(1, virt)
    held = finish(slot_a, part_a, sums, got_a, amps, eps_col, eps_row, occ_a, ())
    residual, updated = finish(slot_b, part_b, sums, got_b, amps, eps_col, eps_row, occ_b, held)
    return (
        residual.reshape(rows_i, 1, virt, virt),
        updated.reshape(rows_i, 1, virt, virt),
    )


def solution(mesh):
    pairs = P("occi", "occj", None, None)
    return jax.shard_map(
        shards,
        mesh=mesh,
        in_specs=(pairs, pairs) + (P(),) * 8,
        out_specs=(pairs, pairs),
        check_vma=False,
    )
```

```python
import functools

import jax
import jax.numpy as jnp
from jax import lax
from jax.experimental import pallas as pl
from jax.experimental.pallas import tpu as pltpu
from jax.sharding import PartitionSpec as P

AXES = ("occi", "occj")
F32 = jnp.float32
BF16 = jnp.bfloat16
SUB = 16


def coupling(fock_occ, couple_list, couple_count):
    n_occ = fock_occ.shape[0]
    slots = jnp.arange(couple_list.shape[1], dtype=jnp.int32)
    active = slots[None, :] < couple_count[:, None]
    target = jnp.arange(n_occ, dtype=jnp.int32)
    hits = (couple_list[:, :, None] == target[None, None, :]) & active[:, :, None]
    return fock_occ * jnp.sum(hits.astype(fock_occ.dtype), axis=1)


def params(limit, **kw):
    return pltpu.CompilerParams(vmem_limit_bytes=limit << 20, **kw)


def whole(shape):
    return pl.BlockSpec(shape, lambda *_: (0,) * len(shape))


def mix_kernel(w_ref, in_ref, out_ref):
    n = in_ref.shape[0]
    w = w_ref[...]
    high = w.astype(BF16)
    rest = w - high.astype(F32)
    mid = rest.astype(BF16)
    low = (rest - mid.astype(F32)).astype(BF16)
    for r in range(0, in_ref.shape[1], SUB):
        rhs = jnp.concatenate([in_ref[k, r : r + SUB, :] for k in range(n)], axis=0)
        total = jnp.dot(high, rhs, preferred_element_type=F32)
        total += jnp.dot(mid, rhs, preferred_element_type=F32)
        total += jnp.dot(low, rhs, preferred_element_type=F32)
        for j in range(n):
            out_ref[j, r : r + SUB, :] = total[j * SUB : (j + 1) * SUB, :].astype(BF16)


def mix(wide, slices):
    return pl.pallas_call(
        mix_kernel,
        out_shape=jax.ShapeDtypeStruct(slices.shape, BF16),
        grid=(1,),
        in_specs=[whole(wide.shape), whole(slices.shape)],
        out_specs=whole(slices.shape),
        compiler_params=params(16),
        cost_estimate=pl.CostEstimate(
            flops=10**9, bytes_accessed=4 * slices.size, transcendentals=0
        ),
        name="mix",
    )(wide, slices)


def ladder_kernel(more, close, slot, amp_ref, x_ref, core_ref, *refs):
    scaled, x_t = refs[-2:]
    refs = refs[:-2]
    step = pl.program_id(0)
    tile = core_ref.shape[1]
    rank = x_ref.shape[1]
    chunk = min(512, rank)
    part_ref = refs[-2] if close else refs[-1]
    amp = amp_ref[...]

    @pl.when(step == 0)
    def _():
        for c in range(0, rank, min(256, rank)):
            cut = slice(c, c + min(256, rank))
            x_t[cut, :] = x_ref[:, cut].T
        if more:
            part_ref[...] = refs[0][...]
        else:
            virtual = jnp.dot(refs[1][...], amp, preferred_element_type=F32)
            part_ref[...] = refs[0][...].astype(F32) + virtual

    here = step + more
    cols = pl.ds(pl.multiple_of(here * tile, tile), tile)
    first = jnp.dot(amp, x_ref[:, cols], preferred_element_type=F32).astype(BF16)
    for p in range(0, rank, chunk):
        middle = jnp.dot(x_t[p : p + chunk, :], first, preferred_element_type=F32)
        scaled[p : p + chunk, :] = (core_ref[p : p + chunk, :].astype(F32) * middle).astype(BF16)
    second = jnp.dot(x_ref[...], scaled[...], preferred_element_type=F32).astype(BF16)
    part_ref[...] += jnp.dot(second, x_t[cols, :], preferred_element_type=F32)
    if close:

        @pl.when(step == pl.num_programs(0) - 1)
        def _():
            half = part_ref[...] - refs[-3][...].astype(F32)
            part_ref[...] = half
            refs[-1][...] = half.astype(BF16)


def ladder(slot, amps, x, core, start, tiles, count, ints=None, fock=None, part=None, sums=None):
    virt, rank = x.shape
    tile = rank // count
    pair = pl.BlockSpec((None, virt, virt), lambda q, s: (s[0], 0, 0))
    square = whole((virt, virt))
    extra, specs = ([part], [square]) if start else ([ints, fock], [pair, square])
    outs, out_specs = [jax.ShapeDtypeStruct((virt, virt), F32)], [square]
    if sums is not None:
        extra, specs = extra + [sums], specs + [pair]
        outs, out_specs = outs + [jax.ShapeDtypeStruct((virt, virt), BF16)], [square, square]
    return pl.pallas_call(
        functools.partial(ladder_kernel, start, sums is not None),
        out_shape=outs,
        grid_spec=pltpu.PrefetchScalarGridSpec(
            num_scalar_prefetch=1,
            grid=(tiles,),
            in_specs=[
                pair,
                whole(x.shape),
                pl.BlockSpec((rank, tile), lambda q, s: (0, q + start)),
            ]
            + specs,
            out_specs=out_specs,
            scratch_shapes=[pltpu.VMEM((rank, tile), BF16), pltpu.VMEM((rank, virt), BF16)],
        ),
        compiler_params=params(54, dimension_semantics=("arbitrary",)),
        cost_estimate=pl.CostEstimate(
            flops=4 * virt * rank * (rank + virt) * tiles // count,
            bytes_accessed=2 * rank * rank * tiles // count + 4 * virt * rank,
            transcendentals=0,
        ),
        name="ladder",
    )(slot, amps, x, core, *extra)


def half_kernel(slot, part_ref, sum_ref, half_ref, send_ref):
    half = part_ref[...] - sum_ref[...].astype(F32)
    half_ref[...] = half
    send_ref[...] = half.astype(BF16)


def half_of(slot, part, sums):
    virt = part.shape[0]
    rows = min(256, virt)
    strip = pl.BlockSpec((rows, virt), lambda r, s: (r, 0))
    return pl.pallas_call(
        half_kernel,
        out_shape=[
            jax.ShapeDtypeStruct(part.shape, F32),
            jax.ShapeDtypeStruct(part.shape, BF16),
        ],
        grid_spec=pltpu.PrefetchScalarGridSpec(
            num_scalar_prefetch=1,
            grid=(virt // rows,),
            in_specs=[strip, pl.BlockSpec((None, rows, virt), lambda r, s: (s[0], r, 0))],
            out_specs=[strip, strip],
        ),
        compiler_params=params(16),
        cost_estimate=pl.CostEstimate(
            flops=0, bytes_accessed=12 * part.size, transcendentals=0
        ),
        name="half",
    )(slot, part, sums)


def finish_kernel(slot, half_ref, mirror_ref, amp_ref, col_ref, row_ref, occ_ref, *refs):
    res_ref, new_ref = refs[-2:]
    residual = half_ref[...] + mirror_ref[...].astype(F32).T
    denominator = col_ref[...] + row_ref[...] - occ_ref[0] - occ_ref[1]
    res_ref[...] = residual
    new_ref[...] = (amp_ref[...].astype(F32) - residual / denominator).astype(BF16)


def finish(slot, half, mirror, amps, eps_col, eps_row, occ, held):
    virt = half.shape[0]
    rows = min(256, virt)
    strip = pl.BlockSpec((None, rows, virt), lambda r, s: (s[0], r, 0))
    held_specs = [pl.BlockSpec(memory_space=pl.ANY)] * len(held)
    return pl.pallas_call(
        finish_kernel,
        out_shape=[
            jax.ShapeDtypeStruct(amps.shape, F32),
            jax.ShapeDtypeStruct(amps.shape, BF16),
        ],
        grid_spec=pltpu.PrefetchScalarGridSpec(
            num_scalar_prefetch=1,
            grid=(virt // rows,),
            in_specs=[
                pl.BlockSpec((rows, virt), lambda r, s: (r, 0)),
                pl.BlockSpec((virt, rows), lambda r, s: (0, r)),
                strip,
                pl.BlockSpec((rows, 1), lambda r, s: (r, 0)),
                whole((1, virt)),
                pl.BlockSpec(memory_space=pltpu.SMEM),
            ]
            + held_specs,
            out_specs=[strip, strip],
        ),
        input_output_aliases={7 + n: n for n in range(len(held))},
        compiler_params=params(16, dimension_semantics=("arbitrary",)),
        cost_estimate=pl.CostEstimate(
            flops=20 * half.size, bytes_accessed=14 * half.size, transcendentals=0
        ),
        name="finish",
    )(slot, half, mirror, amps, eps_col, eps_row, occ, *held)


def shards(
    amplitudes,
    exch_int,
    thc_factor,
    thc_core,
    fock_vir,
    eps_vir,
    eps_occ,
    fock_occ,
    couple_list,
    couple_count,
):
    rows_i, _, virt, _ = amplitudes.shape
    n_first = lax.axis_size("occi")
    n_second = lax.axis_size("occj")
    me_i = lax.axis_index("occi")
    me_j = lax.axis_index("occj")
    core = me_j % 2
    place = jnp.stack([core, me_j // 2]).astype(jnp.int32)
    slot_a = jnp.reshape(core, (1,)).astype(jnp.int32)
    slot_b = 1 - slot_a
    amps = amplitudes.reshape(rows_i, virt, virt)
    ints = exch_int.reshape(rows_i, virt, virt)

    def mirror_hop(flip):
        return [
            (p * n_second + 2 * q + s, q * n_second + 2 * p + (s ^ flip))
            for p in range(n_first)
            for q in range(n_first)
            for s in range(2)
        ]

    slices = amps.reshape(n_second, rows_i * virt // n_second, virt)
    slices = lax.all_to_all(slices, "occj", 0, 0, tiled=True)
    weights = coupling(fock_occ, couple_list, couple_count)
    tall = jnp.repeat(jnp.repeat(weights, SUB, axis=0), SUB, axis=1)
    lane = jnp.arange(n_second * SUB, dtype=jnp.int32) % SUB
    wide = jnp.where(lane[:, None] == lane[None, :], tall, 0.0)
    count = 4
    early = count // 2
    (part_a,) = ladder(
        slot_a, amps, thc_factor, thc_core, 0, early, count, ints=ints, fock=fock_vir
    )
    slices, part_a = lax.optimization_barrier((slices, part_a))
    sums = mix(wide, slices)
    sums, part_a = lax.optimization_barrier((sums, part_a))
    sums = lax.all_to_all(sums, "occj", 0, 0, tiled=True)
    (part_a,) = ladder(
        slot_a, amps, thc_factor, thc_core, early, count - early, count, part=part_a
    )
    sums, part_a = lax.optimization_barrier((sums, part_a))
    sums = sums.reshape(rows_i, virt, virt)
    half_a, send_a = half_of(slot_a, part_a, sums)
    send_a, sums = lax.optimization_barrier((send_a, sums))
    got_a = lax.ppermute(send_a, AXES, mirror_hop(0))
    half_b, send_b = ladder(
        slot_b, amps, thc_factor, thc_core, 0, count, count, ints=ints, fock=fock_vir, sums=sums
    )
    got_b = lax.ppermute(send_b, AXES, mirror_hop(1))

    occ_rows = lax.dynamic_slice_in_dim(eps_occ, me_i * rows_i, rows_i, 0)
    occ_column = lax.dynamic_slice_in_dim(eps_occ, me_j, 1, 0)
    occ_a = jnp.stack([jnp.where(core == 0, occ_rows[0], occ_rows[1]), occ_column[0]])
    occ_b = jnp.stack([jnp.where(core == 0, occ_rows[1], occ_rows[0]), occ_column[0]])
    eps_col = eps_vir.reshape(virt, 1)
    eps_row = eps_vir.reshape(1, virt)
    held = finish(slot_a, half_a, got_a, amps, eps_col, eps_row, occ_a, ())
    residual, updated = finish(slot_b, half_b, got_b, amps, eps_col, eps_row, occ_b, held)
    return (
        residual.reshape(rows_i, 1, virt, virt),
        updated.reshape(rows_i, 1, virt, virt),
    )


def solution(mesh):
    pairs = P("occi", "occj", None, None)
    return jax.shard_map(
        shards,
        mesh=mesh,
        in_specs=(pairs, pairs) + (P(),) * 8,
        out_specs=(pairs, pairs),
        check_vma=False,
    )
```

```python
import functools

import jax
import jax.numpy as jnp
from jax import lax
from jax.experimental import pallas as pl
from jax.experimental.pallas import tpu as pltpu
from jax.sharding import PartitionSpec as P

AXES = ("occi", "occj")
F32 = jnp.float32
BF16 = jnp.bfloat16
SUB = 16


def coupling(fock_occ, couple_list, couple_count):
    n_occ = fock_occ.shape[0]
    slots = jnp.arange(couple_list.shape[1], dtype=jnp.int32)
    active = slots[None, :] < couple_count[:, None]
    target = jnp.arange(n_occ, dtype=jnp.int32)
    hits = (couple_list[:, :, None] == target[None, None, :]) & active[:, :, None]
    return fock_occ * jnp.sum(hits.astype(fock_occ.dtype), axis=1)


def params(limit, **kw):
    return pltpu.CompilerParams(vmem_limit_bytes=limit << 20, **kw)


def whole(shape):
    return pl.BlockSpec(shape, lambda *_: (0,) * len(shape))


def mix_kernel(w_ref, in_ref, out_ref):
    n = in_ref.shape[0]
    w = w_ref[...]
    high = w.astype(BF16)
    rest = w - high.astype(F32)
    mid = rest.astype(BF16)
    low = (rest - mid.astype(F32)).astype(BF16)
    for r in range(0, in_ref.shape[1], SUB):
        rhs = jnp.concatenate([in_ref[k, r : r + SUB, :] for k in range(n)], axis=0)
        total = jnp.dot(high, rhs, preferred_element_type=F32)
        total += jnp.dot(mid, rhs, preferred_element_type=F32)
        total += jnp.dot(low, rhs, preferred_element_type=F32)
        for j in range(n):
            out_ref[j, r : r + SUB, :] = total[j * SUB : (j + 1) * SUB, :].astype(BF16)


def mix(wide, slices):
    return pl.pallas_call(
        mix_kernel,
        out_shape=jax.ShapeDtypeStruct(slices.shape, BF16),
        grid=(1,),
        in_specs=[whole(wide.shape), whole(slices.shape)],
        out_specs=whole(slices.shape),
        compiler_params=params(16),
        cost_estimate=pl.CostEstimate(
            flops=10**9, bytes_accessed=4 * slices.size, transcendentals=0
        ),
        name="mix",
    )(wide, slices)


def ladder_kernel(more, close, slot, amp_ref, x_ref, core_ref, *refs):
    scaled, x_t = refs[-2:]
    refs = refs[:-2]
    step = pl.program_id(0)
    tile = core_ref.shape[1]
    rank = x_ref.shape[1]
    chunk = min(512, rank)
    part_ref = refs[-2] if close else refs[-1]
    amp = amp_ref[...]

    @pl.when(step == 0)
    def _():
        for c in range(0, rank, min(256, rank)):
            cut = slice(c, c + min(256, rank))
            x_t[cut, :] = x_ref[:, cut].T
        if more:
            part_ref[...] = refs[0][...]
        else:
            virtual = jnp.dot(refs[1][...], amp, preferred_element_type=F32)
            part_ref[...] = refs[0][...].astype(F32) + virtual

    here = step + more
    cols = pl.ds(pl.multiple_of(here * tile, tile), tile)
    first = jnp.dot(amp, x_ref[:, cols], preferred_element_type=F32).astype(BF16)
    for p in range(0, rank, chunk):
        middle = jnp.dot(x_t[p : p + chunk, :], first, preferred_element_type=F32)
        scaled[p : p + chunk, :] = (core_ref[p : p + chunk, :].astype(F32) * middle).astype(BF16)
    second = jnp.dot(x_ref[...], scaled[...], preferred_element_type=F32).astype(BF16)
    part_ref[...] += jnp.dot(second, x_t[cols, :], preferred_element_type=F32)
    if close:

        @pl.when(step == pl.num_programs(0) - 1)
        def _():
            half = part_ref[...] - refs[-3][...].astype(F32)
            part_ref[...] = half
            refs[-1][...] = half.astype(BF16)


def ladder(slot, amps, x, core, start, tiles, count, ints=None, fock=None, part=None, sums=None):
    virt, rank = x.shape
    tile = rank // count
    pair = pl.BlockSpec((None, virt, virt), lambda q, s: (s[0], 0, 0))
    square = whole((virt, virt))
    extra, specs = ([part], [square]) if start else ([ints, fock], [pair, square])
    outs, out_specs = [jax.ShapeDtypeStruct((virt, virt), F32)], [square]
    if sums is not None:
        extra, specs = extra + [sums], specs + [pair]
        outs, out_specs = outs + [jax.ShapeDtypeStruct((virt, virt), BF16)], [square, square]
    return pl.pallas_call(
        functools.partial(ladder_kernel, start, sums is not None),
        out_shape=outs,
        grid_spec=pltpu.PrefetchScalarGridSpec(
            num_scalar_prefetch=1,
            grid=(tiles,),
            in_specs=[
                pair,
                whole(x.shape),
                pl.BlockSpec((rank, tile), lambda q, s: (0, q + start)),
            ]
            + specs,
            out_specs=out_specs,
            scratch_shapes=[pltpu.VMEM((rank, tile), BF16), pltpu.VMEM((rank, virt), BF16)],
        ),
        compiler_params=params(54, dimension_semantics=("arbitrary",)),
        cost_estimate=pl.CostEstimate(
            flops=4 * virt * rank * (rank + virt) * tiles // count,
            bytes_accessed=2 * rank * rank * tiles // count + 4 * virt * rank,
            transcendentals=0,
        ),
        name="ladder",
    )(slot, amps, x, core, *extra)


def half_kernel(slot, part_ref, sum_ref, half_ref, send_ref):
    half = part_ref[...] - sum_ref[...].astype(F32)
    half_ref[...] = half
    send_ref[...] = half.astype(BF16)


def half_of(slot, part, sums):
    virt = part.shape[0]
    rows = min(256, virt)
    strip = pl.BlockSpec((rows, virt), lambda r, s: (r, 0))
    return pl.pallas_call(
        half_kernel,
        out_shape=[
            jax.ShapeDtypeStruct(part.shape, F32),
            jax.ShapeDtypeStruct(part.shape, BF16),
        ],
        grid_spec=pltpu.PrefetchScalarGridSpec(
            num_scalar_prefetch=1,
            grid=(virt // rows,),
            in_specs=[strip, pl.BlockSpec((None, rows, virt), lambda r, s: (s[0], r, 0))],
            out_specs=[strip, strip],
        ),
        compiler_params=params(56),
        cost_estimate=pl.CostEstimate(
            flops=0, bytes_accessed=12 * part.size, transcendentals=0
        ),
        name="half",
    )(slot, part, sums)


def finish_kernel(n, ids, half_ref, amp_ref, col_ref, row_ref, occ_ref, *refs):
    res_ref, new_ref = refs[-2:]
    mirror = refs[0][...]
    if n == 2:
        mirror = jnp.where(ids[3] == 1, refs[1][...], mirror)
    residual = half_ref[...] + mirror.astype(F32).T
    denominator = col_ref[...] + row_ref[...] - occ_ref[ids[1]] - occ_ref[ids[2]]
    res_ref[...] = residual
    new_ref[...] = (amp_ref[...].astype(F32) - residual / denominator).astype(BF16)


def finish(ids, half, mirrors, amps, eps_col, eps_row, eps_occ, held):
    virt = half.shape[0]
    rows = min(256, virt)
    strip = pl.BlockSpec((None, rows, virt), lambda r, s: (s[0], r, 0))
    n = len(mirrors)
    return pl.pallas_call(
        functools.partial(finish_kernel, n),
        out_shape=[
            jax.ShapeDtypeStruct(amps.shape, F32),
            jax.ShapeDtypeStruct(amps.shape, BF16),
        ],
        grid_spec=pltpu.PrefetchScalarGridSpec(
            num_scalar_prefetch=1,
            grid=(virt // rows,),
            in_specs=[
                pl.BlockSpec((rows, virt), lambda r, s: (r, 0)),
                strip,
                pl.BlockSpec((rows, 1), lambda r, s: (r, 0)),
                whole((1, virt)),
                pl.BlockSpec(memory_space=pltpu.SMEM),
            ]
            + [pl.BlockSpec((virt, rows), lambda r, s: (0, r))] * n
            + [pl.BlockSpec(memory_space=pl.ANY)] * len(held),
            out_specs=[strip, strip],
        ),
        input_output_aliases={6 + n + m: m for m in range(len(held))},
        compiler_params=params(16, dimension_semantics=("arbitrary",)),
        cost_estimate=pl.CostEstimate(
            flops=20 * half.size, bytes_accessed=14 * half.size, transcendentals=0
        ),
        name="finish",
    )(ids, half, amps, eps_col, eps_row, eps_occ, *mirrors, *held)


def shards(
    amplitudes,
    exch_int,
    thc_factor,
    thc_core,
    fock_vir,
    eps_vir,
    eps_occ,
    fock_occ,
    couple_list,
    couple_count,
):
    rows_i, _, virt, _ = amplitudes.shape
    n_first = lax.axis_size("occi")
    n_second = lax.axis_size("occj")
    me_i = lax.axis_index("occi")
    me_j = lax.axis_index("occj")
    core = me_j % 2
    slot_a = jnp.reshape(core, (1,)).astype(jnp.int32)
    slot_b = 1 - slot_a
    amps = amplitudes.reshape(rows_i, virt, virt)
    ints = exch_int.reshape(rows_i, virt, virt)

    def hop(kind, flip):
        pairs = []
        for y in range(n_first // 2):
            for x in range(n_first // 2):
                far = (x - y) % (n_first // 2) == n_first // 4
                if kind != "all" and far == (kind == "near"):
                    continue
                for low in range(2):
                    for high in range(2):
                        here, over = (y, low, x, high), (x, high, y, low)
                        relay = (x, low, x, high)
                        one, two = {
                            "near": (here, over),
                            "all": (here, over),
                            "to": (here, relay),
                            "from": (relay, over),
                        }[kind]
                        for c in range(2):
                            pairs.append((spot(one, c), spot(two, c ^ flip)))
        return pairs

    def spot(chip, c):
        y, low, x, high = chip
        return (2 * y + low) * n_second + 2 * (2 * x + high) + c

    def send(array, kind, flip):
        return lax.ppermute(array, AXES, hop(kind, flip))

    far_here = ((me_j // 4 - me_i // 2) % (n_first // 2) == n_first // 4).astype(jnp.int32)
    eps_col = eps_vir.reshape(virt, 1)
    eps_row = eps_vir.reshape(1, virt)

    def ids_of(slot):
        return jnp.stack([slot[0], me_i * rows_i + slot[0], me_j, far_here]).astype(jnp.int32)

    ids_a, ids_b = ids_of(slot_a), ids_of(slot_b)

    slices = amps.reshape(n_second, rows_i * virt // n_second, virt)
    slices = lax.all_to_all(slices, "occj", 0, 0, tiled=True)
    weights = coupling(fock_occ, couple_list, couple_count)
    tall = jnp.repeat(jnp.repeat(weights, SUB, axis=0), SUB, axis=1)
    lane = jnp.arange(n_second * SUB, dtype=jnp.int32) % SUB
    wide = jnp.where(lane[:, None] == lane[None, :], tall, 0.0)
    count = 4
    early = count - 1
    tables = (thc_factor, thc_core)
    origin = dict(ints=ints, fock=fock_vir)
    (part_a,) = ladder(slot_a, amps, *tables, 0, count, count, **origin)
    slices, part_a, ids_a, ids_b, eps_col = lax.optimization_barrier(
        (slices, part_a, ids_a, ids_b, eps_col)
    )
    sums = mix(wide, slices)
    sums, part_a, slot_b = lax.optimization_barrier((sums, part_a, slot_b))
    sums = lax.all_to_all(sums, "occj", 0, 0, tiled=True)
    (part_b,) = ladder(slot_b, amps, *tables, 0, early, count, **origin)
    sums, part_a, part_b = lax.optimization_barrier((sums, part_a, part_b))
    sums = sums.reshape(rows_i, virt, virt)
    half_a, send_a = half_of(slot_a, part_a, sums)
    send_a, sums, part_b = lax.optimization_barrier((send_a, sums, part_b))
    near_a = send(send_a, "near", 0)
    relay_a = send(send_a, "to", 0)
    half_b, send_b = ladder(
        slot_b, amps, *tables, early, count - early, count, part=part_b, sums=sums
    )
    got_b = send(send_b, "all", 1)
    relay_a, _ = lax.optimization_barrier((relay_a, send_b))
    far_a = send(relay_a, "from", 0)

    held = finish(ids_a, half_a, (near_a, far_a), amps, eps_col, eps_row, eps_occ, ())
    residual, updated = finish(
        ids_b, half_b, (got_b,), amps, eps_col, eps_row, eps_occ, held
    )
    return (
        residual.reshape(rows_i, 1, virt, virt),
        updated.reshape(rows_i, 1, virt, virt),
    )


def solution(mesh):
    pairs = P("occi", "occj", None, None)
    return jax.shard_map(
        shards,
        mesh=mesh,
        in_specs=(pairs, pairs) + (P(),) * 8,
        out_specs=(pairs, pairs),
        check_vma=False,
    )
```

```python
import functools

import jax
import jax.numpy as jnp
from jax import lax
from jax.experimental import pallas as pl
from jax.experimental.pallas import tpu as pltpu
from jax.sharding import PartitionSpec as P

AXES = ("occi", "occj")
F32 = jnp.float32
BF16 = jnp.bfloat16
SUB = 16


def coupling(fock_occ, couple_list, couple_count):
    n_occ = fock_occ.shape[0]
    slots = jnp.arange(couple_list.shape[1], dtype=jnp.int32)
    active = slots[None, :] < couple_count[:, None]
    target = jnp.arange(n_occ, dtype=jnp.int32)
    hits = (couple_list[:, :, None] == target[None, None, :]) & active[:, :, None]
    return fock_occ * jnp.sum(hits.astype(fock_occ.dtype), axis=1)


def params(limit, **kw):
    return pltpu.CompilerParams(vmem_limit_bytes=limit << 20, **kw)


def whole(shape):
    return pl.BlockSpec(shape, lambda *_: (0,) * len(shape))


def mix_kernel(w_ref, in_ref, out_ref):
    n = in_ref.shape[0]
    w = w_ref[...]
    high = w.astype(BF16)
    rest = w - high.astype(F32)
    mid = rest.astype(BF16)
    low = (rest - mid.astype(F32)).astype(BF16)
    for r in range(0, in_ref.shape[1], SUB):
        rhs = jnp.concatenate([in_ref[k, r : r + SUB, :] for k in range(n)], axis=0)
        total = jnp.dot(high, rhs, preferred_element_type=F32)
        total += jnp.dot(mid, rhs, preferred_element_type=F32)
        total += jnp.dot(low, rhs, preferred_element_type=F32)
        for j in range(n):
            out_ref[j, r : r + SUB, :] = total[j * SUB : (j + 1) * SUB, :].astype(BF16)


def mix(wide, slices):
    return pl.pallas_call(
        mix_kernel,
        out_shape=jax.ShapeDtypeStruct(slices.shape, BF16),
        grid=(1,),
        in_specs=[whole(wide.shape), whole(slices.shape)],
        out_specs=whole(slices.shape),
        compiler_params=params(16),
        cost_estimate=pl.CostEstimate(
            flops=10**9, bytes_accessed=4 * slices.size, transcendentals=0
        ),
        name="mix",
    )(wide, slices)


def ladder_kernel(slot, amp_ref, int_ref, x_ref, core_ref, fock_ref, out_ref, scaled, x_t):
    step = pl.program_id(0)
    tile = core_ref.shape[1]
    rank = x_ref.shape[1]
    chunk = min(512, rank)
    amp = amp_ref[...]

    @pl.when(step == 0)
    def _():
        for c in range(0, rank, min(256, rank)):
            cut = slice(c, c + min(256, rank))
            x_t[cut, :] = x_ref[:, cut].T
        virtual = jnp.dot(fock_ref[...], amp, preferred_element_type=F32)
        out_ref[...] = int_ref[...].astype(F32) + virtual

    cols = pl.ds(pl.multiple_of(step * tile, tile), tile)
    first = jnp.dot(amp, x_ref[:, cols], preferred_element_type=F32).astype(BF16)
    for p in range(0, rank, chunk):
        middle = jnp.dot(x_t[p : p + chunk, :], first, preferred_element_type=F32)
        scaled[p : p + chunk, :] = (core_ref[p : p + chunk, :].astype(F32) * middle).astype(BF16)
    second = jnp.dot(x_ref[...], scaled[...], preferred_element_type=F32).astype(BF16)
    out_ref[...] += jnp.dot(second, x_t[cols, :], preferred_element_type=F32)


def ladder(slot, amps, ints, x, core, fock):
    virt, rank = x.shape
    tile = min(512, rank)
    pair = pl.BlockSpec((None, virt, virt), lambda q, s: (s[0], 0, 0))
    return pl.pallas_call(
        ladder_kernel,
        out_shape=jax.ShapeDtypeStruct((virt, virt), F32),
        grid_spec=pltpu.PrefetchScalarGridSpec(
            num_scalar_prefetch=1,
            grid=(rank // tile,),
            in_specs=[
                pair,
                pair,
                whole(x.shape),
                pl.BlockSpec((rank, tile), lambda q, s: (0, q)),
                whole(fock.shape),
            ],
            out_specs=whole((virt, virt)),
            scratch_shapes=[pltpu.VMEM((rank, tile), BF16), pltpu.VMEM((rank, virt), BF16)],
        ),
        compiler_params=params(54, dimension_semantics=("arbitrary",)),
        cost_estimate=pl.CostEstimate(
            flops=4 * virt * rank * (rank + virt) + 2 * virt**3,
            bytes_accessed=2 * rank * rank + 4 * virt * rank,
            transcendentals=0,
        ),
        name="ladder",
    )(slot, amps, ints, x, core, fock)


def half_kernel(slot, part_a, part_b, sum_ref, send_a, send_b):
    core = slot[0]
    send_a[...] = (part_a[...] - sum_ref[core].astype(F32)).astype(BF16)
    send_b[...] = (part_b[...] - sum_ref[1 - core].astype(F32)).astype(BF16)


def half_of(slot, part_a, part_b, sums):
    virt = part_a.shape[0]
    rows = min(256, virt)
    strip = pl.BlockSpec((rows, virt), lambda r, s: (r, 0))
    return pl.pallas_call(
        half_kernel,
        out_shape=[jax.ShapeDtypeStruct(part_a.shape, BF16)] * 2,
        grid_spec=pltpu.PrefetchScalarGridSpec(
            num_scalar_prefetch=1,
            grid=(virt // rows,),
            in_specs=[strip, strip, pl.BlockSpec((2, rows, virt), lambda r, s: (0, r, 0))],
            out_specs=[strip, strip],
        ),
        compiler_params=params(16),
        cost_estimate=pl.CostEstimate(
            flops=0, bytes_accessed=16 * part_a.size, transcendentals=0
        ),
        name="half",
    )(slot, part_a, part_b, sums)


def finish_kernel(n, ids, part_ref, sum_ref, amp_ref, col_ref, row_ref, occ_ref, *refs):
    res_ref, new_ref = refs[-2:]
    mirror = refs[0][...]
    for kind in range(1, n):
        mirror = jnp.where(ids[3] == kind, refs[kind][...], mirror)
    half = part_ref[...] - sum_ref[...].astype(F32)
    residual = half + mirror.astype(F32).T
    denominator = col_ref[...] + row_ref[...] - occ_ref[ids[1]] - occ_ref[ids[2]]
    res_ref[...] = residual
    new_ref[...] = (amp_ref[...].astype(F32) - residual / denominator).astype(BF16)


def finish(ids, part, sums, mirrors, amps, eps_col, eps_row, eps_occ, held):
    virt = part.shape[0]
    rows = min(256, virt)
    strip = pl.BlockSpec((None, rows, virt), lambda r, s: (s[0], r, 0))
    n = len(mirrors)
    return pl.pallas_call(
        functools.partial(finish_kernel, n),
        out_shape=[
            jax.ShapeDtypeStruct(amps.shape, F32),
            jax.ShapeDtypeStruct(amps.shape, BF16),
        ],
        grid_spec=pltpu.PrefetchScalarGridSpec(
            num_scalar_prefetch=1,
            grid=(virt // rows,),
            in_specs=[
                pl.BlockSpec((rows, virt), lambda r, s: (r, 0)),
                strip,
                strip,
                pl.BlockSpec((rows, 1), lambda r, s: (r, 0)),
                whole((1, virt)),
                pl.BlockSpec(memory_space=pltpu.SMEM),
            ]
            + [pl.BlockSpec((virt, rows), lambda r, s: (0, r))] * n
            + [pl.BlockSpec(memory_space=pl.ANY)] * len(held),
            out_specs=[strip, strip],
        ),
        input_output_aliases={7 + n + m: m for m in range(len(held))},
        compiler_params=params(16, dimension_semantics=("arbitrary",)),
        cost_estimate=pl.CostEstimate(
            flops=20 * part.size, bytes_accessed=14 * part.size, transcendentals=0
        ),
        name="finish",
    )(ids, part, sums, amps, eps_col, eps_row, eps_occ, *mirrors, *held)


def shards(
    amplitudes,
    exch_int,
    thc_factor,
    thc_core,
    fock_vir,
    eps_vir,
    eps_occ,
    fock_occ,
    couple_list,
    couple_count,
):
    rows_i, _, virt, _ = amplitudes.shape
    n_first = lax.axis_size("occi")
    n_second = lax.axis_size("occj")
    me_i = lax.axis_index("occi")
    me_j = lax.axis_index("occj")
    core = me_j % 2
    slot_a = jnp.reshape(core, (1,)).astype(jnp.int32)
    slot_b = 1 - slot_a
    amps = amplitudes.reshape(rows_i, virt, virt)
    ints = exch_int.reshape(rows_i, virt, virt)

    size = n_first // 2

    def spot(y, low, x, high, c):
        return (2 * y + low) * n_second + 2 * (2 * x + high) + c

    def send(array, flip, diagonal=None, middle=None, other=None):
        pairs = []
        for y in range(size):
            for x in range(size):
                apart = (x - y) % size
                route = {0: diagonal, size // 2: middle}.get(apart, other)
                for low in range(2):
                    for high in range(2):
                        for c in range(2):
                            ends = dict(
                                mirror=((y, low, x, high), (x, high, y, low)),
                                inward=((y, low, x, high), (x, low, x, high)),
                                outward=((x, low, x, high), (x, high, y, low)),
                            ).get(route)
                            if ends:
                                pairs.append((spot(*ends[0], c), spot(*ends[1], c ^ flip)))
        return lax.ppermute(array, AXES, pairs)

    apart = (me_j // 4 - me_i // 2) % size
    kind = jnp.where(apart == size // 2, 1, jnp.where(apart == 0, 2, 0))
    eps_col = eps_vir.reshape(virt, 1)
    eps_row = eps_vir.reshape(1, virt)

    def ids_of(slot):
        return jnp.stack([slot[0], me_i * rows_i + slot[0], me_j, kind]).astype(jnp.int32)

    ids_a, ids_b = ids_of(slot_a), ids_of(slot_b)

    slices = amps.reshape(n_second, rows_i * virt // n_second, virt)
    slices = lax.all_to_all(slices, "occj", 0, 0, tiled=True)
    weights = coupling(fock_occ, couple_list, couple_count)
    tall = jnp.repeat(jnp.repeat(weights, SUB, axis=0), SUB, axis=1)
    lane = jnp.arange(n_second * SUB, dtype=jnp.int32) % SUB
    wide = jnp.where(lane[:, None] == lane[None, :], tall, 0.0)
    part_a = ladder(slot_a, amps, ints, thc_factor, thc_core, fock_vir)
    slices, part_a, ids_a, ids_b, eps_col = lax.optimization_barrier(
        (slices, part_a, ids_a, ids_b, eps_col)
    )
    sums = mix(wide, slices)
    sums, part_a, slot_b = lax.optimization_barrier((sums, part_a, slot_b))
    sums = lax.all_to_all(sums, "occj", 0, 0, tiled=True)
    part_b = ladder(slot_b, amps, ints, thc_factor, thc_core, fock_vir)
    sums, part_b = lax.optimization_barrier((sums, part_b))
    sums = sums.reshape(rows_i, virt, virt)
    send_a, send_b = half_of(slot_a, part_a, part_b, sums)
    near_a = send(send_a, 0, middle="inward", other="mirror")
    got_b = send(send_b, 1, diagonal="mirror", middle="mirror", other="mirror")
    same_a = send(send_a, 0, diagonal="mirror")
    far_a = send(near_a, 0, middle="outward")

    held = finish(ids_b, part_b, sums, (got_b,), amps, eps_col, eps_row, eps_occ, ())
    residual, updated = finish(
        ids_a, part_a, sums, (near_a, far_a, same_a), amps, eps_col, eps_row, eps_occ, held
    )
    return (
        residual.reshape(rows_i, 1, virt, virt),
        updated.reshape(rows_i, 1, virt, virt),
    )


def solution(mesh):
    pairs = P("occi", "occj", None, None)
    return jax.shard_map(
        shards,
        mesh=mesh,
        in_specs=(pairs, pairs) + (P(),) * 8,
        out_specs=(pairs, pairs),
        check_vma=False,
    )
```

```python
import functools

import jax
import jax.numpy as jnp
from jax import lax
from jax.experimental import pallas as pl
from jax.experimental.pallas import tpu as pltpu
from jax.sharding import PartitionSpec as P

AXES = ("occi", "occj")
F32 = jnp.float32
BF16 = jnp.bfloat16
SUB = 16


def coupling(fock_occ, couple_list, couple_count):
    n_occ = fock_occ.shape[0]
    slots = jnp.arange(couple_list.shape[1], dtype=jnp.int32)
    active = slots[None, :] < couple_count[:, None]
    target = jnp.arange(n_occ, dtype=jnp.int32)
    hits = (couple_list[:, :, None] == target[None, None, :]) & active[:, :, None]
    return fock_occ * jnp.sum(hits.astype(fock_occ.dtype), axis=1)


def params(limit, **kw):
    return pltpu.CompilerParams(vmem_limit_bytes=limit << 20, **kw)


def whole(shape):
    return pl.BlockSpec(shape, lambda *_: (0,) * len(shape))


def mix_kernel(w_ref, in_ref, out_ref):
    n = in_ref.shape[0]
    w = w_ref[...]
    high = w.astype(BF16)
    rest = w - high.astype(F32)
    mid = rest.astype(BF16)
    low = (rest - mid.astype(F32)).astype(BF16)
    for r in range(0, in_ref.shape[1], SUB):
        rhs = jnp.concatenate([in_ref[k, r : r + SUB, :] for k in range(n)], axis=0)
        total = jnp.dot(high, rhs, preferred_element_type=F32)
        total += jnp.dot(mid, rhs, preferred_element_type=F32)
        total += jnp.dot(low, rhs, preferred_element_type=F32)
        for j in range(n):
            out_ref[j, r : r + SUB, :] = total[j * SUB : (j + 1) * SUB, :].astype(BF16)


def mix(wide, slices):
    return pl.pallas_call(
        mix_kernel,
        out_shape=jax.ShapeDtypeStruct(slices.shape, BF16),
        grid=(1,),
        in_specs=[whole(wide.shape), whole(slices.shape)],
        out_specs=whole(slices.shape),
        compiler_params=params(16),
        cost_estimate=pl.CostEstimate(
            flops=10**9, bytes_accessed=4 * slices.size, transcendentals=0
        ),
        name="mix",
    )(wide, slices)


def ladder_kernel(slot, amp_ref, int_ref, x_ref, core_ref, fock_ref, out_ref, scaled, x_t):
    step = pl.program_id(0)
    tile = core_ref.shape[1]
    rank = x_ref.shape[1]
    chunk = min(512, rank)
    amp = amp_ref[...]

    @pl.when(step == 0)
    def _():
        for c in range(0, rank, min(256, rank)):
            cut = slice(c, c + min(256, rank))
            x_t[cut, :] = x_ref[:, cut].T
        virtual = jnp.dot(fock_ref[...], amp, preferred_element_type=F32)
        out_ref[...] = int_ref[...].astype(F32) + virtual

    cols = pl.ds(pl.multiple_of(step * tile, tile), tile)
    first = jnp.dot(amp, x_ref[:, cols], preferred_element_type=F32).astype(BF16)
    for p in range(0, rank, chunk):
        middle = jnp.dot(x_t[p : p + chunk, :], first, preferred_element_type=F32)
        scaled[p : p + chunk, :] = (core_ref[p : p + chunk, :].astype(F32) * middle).astype(BF16)
    second = jnp.dot(x_ref[...], scaled[...], preferred_element_type=F32).astype(BF16)
    out_ref[...] += jnp.dot(second, x_t[cols, :], preferred_element_type=F32)


def ladder(slot, amps, ints, x, core, fock):
    virt, rank = x.shape
    tile = min(512, rank)
    pair = pl.BlockSpec((None, virt, virt), lambda q, s: (s[0], 0, 0))
    return pl.pallas_call(
        ladder_kernel,
        out_shape=jax.ShapeDtypeStruct((virt, virt), F32),
        grid_spec=pltpu.PrefetchScalarGridSpec(
            num_scalar_prefetch=1,
            grid=(rank // tile,),
            in_specs=[
                pair,
                pair,
                whole(x.shape),
                pl.BlockSpec((rank, tile), lambda q, s: (0, q)),
                whole(fock.shape),
            ],
            out_specs=whole((virt, virt)),
            scratch_shapes=[pltpu.VMEM((rank, tile), BF16), pltpu.VMEM((rank, virt), BF16)],
        ),
        compiler_params=params(54, dimension_semantics=("arbitrary",)),
        cost_estimate=pl.CostEstimate(
            flops=4 * virt * rank * (rank + virt) + 2 * virt**3,
            bytes_accessed=2 * rank * rank + 4 * virt * rank,
            transcendentals=0,
        ),
        name="ladder",
    )(slot, amps, ints, x, core, fock)


def half_kernel(slot, part_a, part_b, sum_ref, send_a, low_b, high_b):
    core = slot[0]
    send_a[...] = (part_a[...] - sum_ref[core].astype(F32)).astype(BF16)
    rounded = (part_b[...] - sum_ref[1 - core].astype(F32)).astype(BF16)

    @pl.when(pl.program_id(0) == 0)
    def _():
        low_b[...] = rounded

    @pl.when(pl.program_id(0) == 1)
    def _():
        high_b[...] = rounded


def half_of(slot, part_a, part_b, sums):
    virt = part_a.shape[0]
    rows = virt // 2
    strip = pl.BlockSpec((rows, virt), lambda r, s: (r, 0))
    return pl.pallas_call(
        half_kernel,
        out_shape=[jax.ShapeDtypeStruct((n, virt), BF16) for n in (virt, rows, rows)],
        grid_spec=pltpu.PrefetchScalarGridSpec(
            num_scalar_prefetch=1,
            grid=(2,),
            in_specs=[strip, strip, pl.BlockSpec((2, rows, virt), lambda r, s: (0, r, 0))],
            out_specs=[strip, whole((rows, virt)), whole((rows, virt))],
        ),
        compiler_params=params(16),
        cost_estimate=pl.CostEstimate(
            flops=0, bytes_accessed=16 * part_a.size, transcendentals=0
        ),
        name="half",
    )(slot, part_a, part_b, sums)


def finish_kernel(counts, ids, part_ref, sum_ref, amp_ref, col_ref, row_ref, occ_ref, *refs):
    res_ref, new_ref = refs[-2:]
    pieces = []
    for n in counts:
        piece = refs[0][...]
        for kind in range(1, n):
            piece = jnp.where(ids[3] == kind, refs[kind][...], piece)
        pieces.append(piece)
        refs = refs[n:]
    mirror = jnp.concatenate(pieces, axis=0)
    half = part_ref[...] - sum_ref[...].astype(F32)
    residual = half + mirror.astype(F32).T
    denominator = col_ref[...] + row_ref[...] - occ_ref[ids[1]] - occ_ref[ids[2]]
    res_ref[...] = residual
    new_ref[...] = (amp_ref[...].astype(F32) - residual / denominator).astype(BF16)


def finish(ids, part, sums, mirrors, amps, eps_col, eps_row, eps_occ, held):
    virt = part.shape[0]
    rows = min(256, virt)
    strip = pl.BlockSpec((None, rows, virt), lambda r, s: (s[0], r, 0))
    counts = [len(piece) for piece in mirrors]
    mirrors = sum(mirrors, ())
    return pl.pallas_call(
        functools.partial(finish_kernel, counts),
        out_shape=[
            jax.ShapeDtypeStruct(amps.shape, F32),
            jax.ShapeDtypeStruct(amps.shape, BF16),
        ],
        grid_spec=pltpu.PrefetchScalarGridSpec(
            num_scalar_prefetch=1,
            grid=(virt // rows,),
            in_specs=[
                pl.BlockSpec((rows, virt), lambda r, s: (r, 0)),
                strip,
                strip,
                pl.BlockSpec((rows, 1), lambda r, s: (r, 0)),
                whole((1, virt)),
                pl.BlockSpec(memory_space=pltpu.SMEM),
            ]
            + [pl.BlockSpec((m.shape[0], rows), lambda r, s: (0, r)) for m in mirrors]
            + [pl.BlockSpec(memory_space=pl.ANY)] * len(held),
            out_specs=[strip, strip],
        ),
        input_output_aliases={7 + sum(counts) + m: m for m in range(len(held))},
        compiler_params=params(16, dimension_semantics=("arbitrary",)),
        cost_estimate=pl.CostEstimate(
            flops=20 * part.size, bytes_accessed=14 * part.size, transcendentals=0
        ),
        name="finish",
    )(ids, part, sums, amps, eps_col, eps_row, eps_occ, *mirrors, *held)


def shards(
    amplitudes,
    exch_int,
    thc_factor,
    thc_core,
    fock_vir,
    eps_vir,
    eps_occ,
    fock_occ,
    couple_list,
    couple_count,
):
    rows_i, _, virt, _ = amplitudes.shape
    n_first = lax.axis_size("occi")
    n_second = lax.axis_size("occj")
    me_i = lax.axis_index("occi")
    me_j = lax.axis_index("occj")
    core = me_j % 2
    slot_a = jnp.reshape(core, (1,)).astype(jnp.int32)
    slot_b = 1 - slot_a
    amps = amplitudes.reshape(rows_i, virt, virt)
    ints = exch_int.reshape(rows_i, virt, virt)

    size = n_first // 2

    def spot(y, low, x, high, c):
        return (2 * y + low) * n_second + 2 * (2 * x + high) + c

    def send(array, flip, diagonal=None, middle=None, other=None):
        pairs = []
        for y in range(size):
            for x in range(size):
                apart = (x - y) % size
                route = {0: diagonal, size // 2: middle}.get(apart, other)
                for low in range(2):
                    for high in range(2):
                        for c in range(2):
                            ends = dict(
                                mirror=((y, low, x, high), (x, high, y, low)),
                                inward=((y, low, x, high), (x, low, x, high)),
                                outward=((x, low, x, high), (x, high, y, low)),
                            ).get(route)
                            if ends:
                                pairs.append((spot(*ends[0], c), spot(*ends[1], c ^ flip)))
        return lax.ppermute(array, AXES, pairs)

    apart = (me_j // 4 - me_i // 2) % size
    kind = jnp.where(apart == size // 2, 1, jnp.where(apart == 0, 2, 0))
    eps_col = eps_vir.reshape(virt, 1)
    eps_row = eps_vir.reshape(1, virt)

    def ids_of(slot):
        return jnp.stack([slot[0], me_i * rows_i + slot[0], me_j, kind]).astype(jnp.int32)

    ids_a, ids_b = ids_of(slot_a), ids_of(slot_b)

    slices = amps.reshape(n_second, rows_i * virt // n_second, virt)
    slices = lax.all_to_all(slices, "occj", 0, 0, tiled=True)
    weights = coupling(fock_occ, couple_list, couple_count)
    tall = jnp.repeat(jnp.repeat(weights, SUB, axis=0), SUB, axis=1)
    lane = jnp.arange(n_second * SUB, dtype=jnp.int32) % SUB
    wide = jnp.where(lane[:, None] == lane[None, :], tall, 0.0)
    part_a = ladder(slot_a, amps, ints, thc_factor, thc_core, fock_vir)
    slices, part_a, ids_a, ids_b, eps_col = lax.optimization_barrier(
        (slices, part_a, ids_a, ids_b, eps_col)
    )
    sums = mix(wide, slices)
    sums, part_a, slot_b = lax.optimization_barrier((sums, part_a, slot_b))
    sums = lax.all_to_all(sums, "occj", 0, 0, tiled=True)
    part_b = ladder(slot_b, amps, ints, thc_factor, thc_core, fock_vir)
    sums, part_b = lax.optimization_barrier((sums, part_b))
    sums = sums.reshape(rows_i, virt, virt)
    send_a, low_b, high_b = half_of(slot_a, part_a, part_b, sums)
    near_a = send(send_a, 0, middle="inward", other="mirror")
    near_b = send(high_b, 1, middle="inward", other="mirror")
    low_b = send(low_b, 1, diagonal="mirror", middle="mirror", other="mirror")
    same_a = send(send_a, 0, diagonal="mirror")
    same_b = send(high_b, 1, diagonal="mirror")
    near_a, low_b = lax.optimization_barrier((near_a, low_b))
    near_b, low_b = lax.optimization_barrier((near_b, low_b))
    far_a = send(near_a, 0, middle="outward")
    far_b = send(near_b, 0, middle="outward")

    far_a, far_b = lax.optimization_barrier((far_a, far_b))
    tables = (amps, eps_col, eps_row, eps_occ)
    mirror_a = [(near_a, far_a, same_a)]
    mirror_b = [(low_b,), (near_b, far_b, same_b)]
    held = finish(ids_a, part_a, sums, mirror_a, *tables, ())
    residual, updated = finish(ids_b, part_b, sums, mirror_b, *tables, held)
    return (
        residual.reshape(rows_i, 1, virt, virt),
        updated.reshape(rows_i, 1, virt, virt),
    )


def solution(mesh):
    pairs = P("occi", "occj", None, None)
    return jax.shard_map(
        shards,
        mesh=mesh,
        in_specs=(pairs, pairs) + (P(),) * 8,
        out_specs=(pairs, pairs),
        check_vma=False,
    )
```

```python
import functools

import jax
import jax.numpy as jnp
from jax import lax
from jax.experimental import pallas as pl
from jax.experimental.pallas import tpu as pltpu
from jax.sharding import PartitionSpec as P

AXES = ("occi", "occj")
F32 = jnp.float32
BF16 = jnp.bfloat16
SUB = 16


def coupling(fock_occ, couple_list, couple_count):
    n_occ = fock_occ.shape[0]
    slots = jnp.arange(couple_list.shape[1], dtype=jnp.int32)
    active = slots[None, :] < couple_count[:, None]
    target = jnp.arange(n_occ, dtype=jnp.int32)
    hits = (couple_list[:, :, None] == target[None, None, :]) & active[:, :, None]
    return fock_occ * jnp.sum(hits.astype(fock_occ.dtype), axis=1)


def params(limit, **kw):
    return pltpu.CompilerParams(vmem_limit_bytes=limit << 20, **kw)


def whole(shape):
    return pl.BlockSpec(shape, lambda *_: (0,) * len(shape))


def mix_kernel(w_ref, in_ref, out_ref):
    n = in_ref.shape[0]
    w = w_ref[...]
    high = w.astype(BF16)
    rest = w - high.astype(F32)
    mid = rest.astype(BF16)
    low = (rest - mid.astype(F32)).astype(BF16)
    for r in range(0, in_ref.shape[1], SUB):
        rhs = jnp.concatenate([in_ref[k, r : r + SUB, :] for k in range(n)], axis=0)
        total = jnp.dot(high, rhs, preferred_element_type=F32)
        total += jnp.dot(mid, rhs, preferred_element_type=F32)
        total += jnp.dot(low, rhs, preferred_element_type=F32)
        for j in range(n):
            out_ref[j, r : r + SUB, :] = total[j * SUB : (j + 1) * SUB, :].astype(BF16)


def mix(wide, slices):
    return pl.pallas_call(
        mix_kernel,
        out_shape=jax.ShapeDtypeStruct(slices.shape, BF16),
        grid=(1,),
        in_specs=[whole(wide.shape), whole(slices.shape)],
        out_specs=whole(slices.shape),
        compiler_params=params(16),
        cost_estimate=pl.CostEstimate(
            flops=10**9, bytes_accessed=4 * slices.size, transcendentals=0
        ),
        name="mix",
    )(wide, slices)


def ladder_kernel(slot, amp_ref, int_ref, x_ref, core_ref, fock_ref, out_ref, scaled, x_t):
    step = pl.program_id(0)
    tile = core_ref.shape[1]
    rank = x_ref.shape[1]
    chunk = min(512, rank)
    amp = amp_ref[...]

    @pl.when(step == 0)
    def _():
        for c in range(0, rank, min(256, rank)):
            cut = slice(c, c + min(256, rank))
            x_t[cut, :] = x_ref[:, cut].T
        virtual = jnp.dot(fock_ref[...], amp, preferred_element_type=F32)
        out_ref[...] = int_ref[...].astype(F32) + virtual

    cols = pl.ds(pl.multiple_of(step * tile, tile), tile)
    first = jnp.dot(amp, x_ref[:, cols], preferred_element_type=F32).astype(BF16)
    for p in range(0, rank, chunk):
        middle = jnp.dot(x_t[p : p + chunk, :], first, preferred_element_type=F32)
        scaled[p : p + chunk, :] = (core_ref[p : p + chunk, :].astype(F32) * middle).astype(BF16)
    second = jnp.dot(x_ref[...], scaled[...], preferred_element_type=F32).astype(BF16)
    out_ref[...] += jnp.dot(second, x_t[cols, :], preferred_element_type=F32)


def ladder(slot, amps, ints, x, core, fock):
    virt, rank = x.shape
    tile = min(512, rank)
    pair = pl.BlockSpec((None, virt, virt), lambda q, s: (s[0], 0, 0))
    return pl.pallas_call(
        ladder_kernel,
        out_shape=jax.ShapeDtypeStruct((virt, virt), F32),
        grid_spec=pltpu.PrefetchScalarGridSpec(
            num_scalar_prefetch=1,
            grid=(rank // tile,),
            in_specs=[
                pair,
                pair,
                whole(x.shape),
                pl.BlockSpec((rank, tile), lambda q, s: (0, q)),
                whole(fock.shape),
            ],
            out_specs=whole((virt, virt)),
            scratch_shapes=[pltpu.VMEM((rank, tile), BF16), pltpu.VMEM((rank, virt), BF16)],
        ),
        compiler_params=params(54, dimension_semantics=("arbitrary",)),
        cost_estimate=pl.CostEstimate(
            flops=4 * virt * rank * (rank + virt) + 2 * virt**3,
            bytes_accessed=2 * rank * rank + 4 * virt * rank,
            transcendentals=0,
        ),
        name="ladder",
    )(slot, amps, ints, x, core, fock)


def half_kernel(slot, part_a, part_b, sum_ref, send_a, low_b, high_b):
    core = slot[0]
    send_a[...] = (part_a[...] - sum_ref[core].astype(F32)).astype(BF16)
    rounded = (part_b[...] - sum_ref[1 - core].astype(F32)).astype(BF16)

    @pl.when(pl.program_id(0) == 0)
    def _():
        low_b[...] = rounded

    @pl.when(pl.program_id(0) == 1)
    def _():
        high_b[...] = rounded


def half_of(slot, part_a, part_b, sums):
    virt = part_a.shape[0]
    rows = virt // 2
    strip = pl.BlockSpec((rows, virt), lambda r, s: (r, 0))
    return pl.pallas_call(
        half_kernel,
        out_shape=[jax.ShapeDtypeStruct((n, virt), BF16) for n in (virt, rows, rows)],
        grid_spec=pltpu.PrefetchScalarGridSpec(
            num_scalar_prefetch=1,
            grid=(2,),
            in_specs=[strip, strip, pl.BlockSpec((2, rows, virt), lambda r, s: (0, r, 0))],
            out_specs=[strip, whole((rows, virt)), whole((rows, virt))],
        ),
        compiler_params=params(16),
        cost_estimate=pl.CostEstimate(
            flops=0, bytes_accessed=16 * part_a.size, transcendentals=0
        ),
        name="half",
    )(slot, part_a, part_b, sums)


def finish_kernel(counts, ids, part_ref, sum_ref, amp_ref, col_ref, row_ref, occ_ref, *refs):
    res_ref, new_ref = refs[-2:]
    pieces = []
    for n in counts:
        piece = refs[0][...]
        for kind in range(1, n):
            piece = jnp.where(ids[3] == kind, refs[kind][...], piece)
        pieces.append(piece)
        refs = refs[n:]
    mirror = jnp.concatenate(pieces, axis=0)
    half = part_ref[...] - sum_ref[...].astype(F32)
    residual = half + mirror.astype(F32).T
    denominator = col_ref[...] + row_ref[...] - occ_ref[ids[1]] - occ_ref[ids[2]]
    res_ref[...] = residual
    new_ref[...] = (amp_ref[...].astype(F32) - residual / denominator).astype(BF16)


def finish(ids, part, sums, mirrors, amps, eps_col, eps_row, eps_occ, held):
    virt = part.shape[0]
    rows = min(256, virt)
    strip = pl.BlockSpec((None, rows, virt), lambda r, s: (s[0], r, 0))
    counts = [len(piece) for piece in mirrors]
    mirrors = sum(mirrors, ())
    return pl.pallas_call(
        functools.partial(finish_kernel, counts),
        out_shape=[
            jax.ShapeDtypeStruct(amps.shape, F32),
            jax.ShapeDtypeStruct(amps.shape, BF16),
        ],
        grid_spec=pltpu.PrefetchScalarGridSpec(
            num_scalar_prefetch=1,
            grid=(virt // rows,),
            in_specs=[
                pl.BlockSpec((rows, virt), lambda r, s: (r, 0)),
                strip,
                strip,
                pl.BlockSpec((rows, 1), lambda r, s: (r, 0)),
                whole((1, virt)),
                pl.BlockSpec(memory_space=pltpu.SMEM),
            ]
            + [pl.BlockSpec((m.shape[0], rows), lambda r, s: (0, r)) for m in mirrors]
            + [pl.BlockSpec(memory_space=pl.ANY)] * len(held),
            out_specs=[strip, strip],
        ),
        input_output_aliases={7 + sum(counts) + m: m for m in range(len(held))},
        compiler_params=params(16, dimension_semantics=("arbitrary",)),
        cost_estimate=pl.CostEstimate(
            flops=20 * part.size, bytes_accessed=14 * part.size, transcendentals=0
        ),
        name="finish",
    )(ids, part, sums, amps, eps_col, eps_row, eps_occ, *mirrors, *held)


def shards(
    amplitudes,
    exch_int,
    thc_factor,
    thc_core,
    fock_vir,
    eps_vir,
    eps_occ,
    fock_occ,
    couple_list,
    couple_count,
):
    rows_i, _, virt, _ = amplitudes.shape
    n_first = lax.axis_size("occi")
    n_second = lax.axis_size("occj")
    me_i = lax.axis_index("occi")
    me_j = lax.axis_index("occj")
    core = me_j % 2
    slot_a = jnp.reshape(core, (1,)).astype(jnp.int32)
    slot_b = 1 - slot_a
    amps = amplitudes.reshape(rows_i, virt, virt)
    ints = exch_int.reshape(rows_i, virt, virt)

    size = n_first // 2

    def spot(y, low, x, high, c):
        return (2 * y + low) * n_second + 2 * (2 * x + high) + c

    def send(array, flip, diagonal=None, middle=None, other=None):
        pairs = []
        for y in range(size):
            for x in range(size):
                apart = (x - y) % size
                route = {0: diagonal, size // 2: middle}.get(apart, other)
                for low in range(2):
                    for high in range(2):
                        for c in range(2):
                            ends = dict(
                                mirror=((y, low, x, high), (x, high, y, low)),
                                inward=((y, low, x, high), (x, low, x, high)),
                                outward=((x, low, x, high), (x, high, y, low)),
                            ).get(route)
                            if ends:
                                pairs.append((spot(*ends[0], c), spot(*ends[1], c ^ flip)))
        return lax.ppermute(array, AXES, pairs)

    apart = (me_j // 4 - me_i // 2) % size
    kind = jnp.where(apart == size // 2, 1, jnp.where(apart == 0, 2, 0))
    eps_col = eps_vir.reshape(virt, 1)
    eps_row = eps_vir.reshape(1, virt)

    def ids_of(slot):
        return jnp.stack([slot[0], me_i * rows_i + slot[0], me_j, kind]).astype(jnp.int32)

    ids_a, ids_b = ids_of(slot_a), ids_of(slot_b)

    slices = amps.reshape(n_second, rows_i * virt // n_second, virt)
    slices = lax.all_to_all(slices, "occj", 0, 0, tiled=True)
    weights = coupling(fock_occ, couple_list, couple_count)
    tall = jnp.repeat(jnp.repeat(weights, SUB, axis=0), SUB, axis=1)
    lane = jnp.arange(n_second * SUB, dtype=jnp.int32) % SUB
    wide = jnp.where(lane[:, None] == lane[None, :], tall, 0.0)
    part_a = ladder(slot_a, amps, ints, thc_factor, thc_core, fock_vir)
    slices, part_a, ids_a, ids_b, eps_col = lax.optimization_barrier(
        (slices, part_a, ids_a, ids_b, eps_col)
    )
    sums = mix(wide, slices)
    sums, part_a, slot_b = lax.optimization_barrier((sums, part_a, slot_b))
    sums = lax.all_to_all(sums, "occj", 0, 0, tiled=True)
    part_b = ladder(slot_b, amps, ints, thc_factor, thc_core, fock_vir)
    sums, part_b = lax.optimization_barrier((sums, part_b))
    sums = sums.reshape(rows_i, virt, virt)
    send_a, low_b, high_b = half_of(slot_a, part_a, part_b, sums)
    near_a = send(send_a, 0, middle="inward", other="mirror")
    near_b = send(high_b, 1, middle="inward", other="mirror")
    low_b = send(low_b, 1, diagonal="mirror", middle="mirror", other="mirror")
    same_a = send(send_a, 0, diagonal="mirror")
    same_b = send(high_b, 1, diagonal="mirror")
    near_b, low_b = lax.optimization_barrier((near_b, low_b))
    far_a = send(near_a, 0, middle="outward")
    far_b = send(near_b, 0, middle="outward")

    far_a, far_b = lax.optimization_barrier((far_a, far_b))
    tables = (amps, eps_col, eps_row, eps_occ)
    mirror_a = [(near_a, far_a, same_a)]
    mirror_b = [(low_b,), (near_b, far_b, same_b)]
    held = finish(ids_a, part_a, sums, mirror_a, *tables, ())
    residual, updated = finish(ids_b, part_b, sums, mirror_b, *tables, held)
    return (
        residual.reshape(rows_i, 1, virt, virt),
        updated.reshape(rows_i, 1, virt, virt),
    )


def solution(mesh):
    pairs = P("occi", "occj", None, None)
    return jax.shard_map(
        shards,
        mesh=mesh,
        in_specs=(pairs, pairs) + (P(),) * 8,
        out_specs=(pairs, pairs),
        check_vma=False,
    )
```

```python
import functools

import jax
import jax.numpy as jnp
from jax import lax
from jax.experimental import pallas as pl
from jax.experimental.pallas import tpu as pltpu
from jax.sharding import PartitionSpec as P

AXES = ("occi", "occj")
F32 = jnp.float32
BF16 = jnp.bfloat16
SUB = 16


def coupling(fock_occ, couple_list, couple_count):
    n_occ = fock_occ.shape[0]
    slots = jnp.arange(couple_list.shape[1], dtype=jnp.int32)
    active = slots[None, :] < couple_count[:, None]
    target = jnp.arange(n_occ, dtype=jnp.int32)
    hits = (couple_list[:, :, None] == target[None, None, :]) & active[:, :, None]
    return fock_occ * jnp.sum(hits.astype(fock_occ.dtype), axis=1)


def params(limit, **kw):
    return pltpu.CompilerParams(vmem_limit_bytes=limit << 20, **kw)


def whole(shape):
    return pl.BlockSpec(shape, lambda *_: (0,) * len(shape))


def mix_kernel(w_ref, in_ref, out_ref):
    n = in_ref.shape[0]
    w = w_ref[...]
    high = w.astype(BF16)
    rest = w - high.astype(F32)
    mid = rest.astype(BF16)
    low = (rest - mid.astype(F32)).astype(BF16)
    for r in range(0, in_ref.shape[1], SUB):
        rhs = jnp.concatenate([in_ref[k, r : r + SUB, :] for k in range(n)], axis=0)
        total = jnp.dot(high, rhs, preferred_element_type=F32)
        total += jnp.dot(mid, rhs, preferred_element_type=F32)
        total += jnp.dot(low, rhs, preferred_element_type=F32)
        for j in range(n):
            out_ref[j, r : r + SUB, :] = total[j * SUB : (j + 1) * SUB, :].astype(BF16)


def mix(wide, slices):
    return pl.pallas_call(
        mix_kernel,
        out_shape=jax.ShapeDtypeStruct(slices.shape, BF16),
        grid=(1,),
        in_specs=[whole(wide.shape), whole(slices.shape)],
        out_specs=whole(slices.shape),
        compiler_params=params(16),
        cost_estimate=pl.CostEstimate(
            flops=10**9, bytes_accessed=4 * slices.size, transcendentals=0
        ),
        name="mix",
    )(wide, slices)


def ladder_kernel(slot, amp_ref, int_ref, x_ref, core_ref, fock_ref, out_ref, scaled, x_t):
    step = pl.program_id(0)
    tile = core_ref.shape[1]
    rank = x_ref.shape[1]
    chunk = min(512, rank)
    amp = amp_ref[...]

    @pl.when(step == 0)
    def _():
        for c in range(0, rank, min(256, rank)):
            cut = slice(c, c + min(256, rank))
            x_t[cut, :] = x_ref[:, cut].T
        virtual = jnp.dot(fock_ref[...], amp, preferred_element_type=F32)
        out_ref[...] = int_ref[...].astype(F32) + virtual

    cols = pl.ds(pl.multiple_of(step * tile, tile), tile)
    first = jnp.dot(amp, x_ref[:, cols], preferred_element_type=F32).astype(BF16)
    for p in range(0, rank, chunk):
        middle = jnp.dot(x_t[p : p + chunk, :], first, preferred_element_type=F32)
        scaled[p : p + chunk, :] = (core_ref[p : p + chunk, :].astype(F32) * middle).astype(BF16)
    second = jnp.dot(x_ref[...], scaled[...], preferred_element_type=F32).astype(BF16)
    out_ref[...] += jnp.dot(second, x_t[cols, :], preferred_element_type=F32)


def ladder(slot, amps, ints, x, core, fock):
    virt, rank = x.shape
    tile = min(512, rank)
    pair = pl.BlockSpec((None, virt, virt), lambda q, s: (s[0], 0, 0))
    return pl.pallas_call(
        ladder_kernel,
        out_shape=jax.ShapeDtypeStruct((virt, virt), F32),
        grid_spec=pltpu.PrefetchScalarGridSpec(
            num_scalar_prefetch=1,
            grid=(rank // tile,),
            in_specs=[
                pair,
                pair,
                whole(x.shape),
                pl.BlockSpec((rank, tile), lambda q, s: (0, q)),
                whole(fock.shape),
            ],
            out_specs=whole((virt, virt)),
            scratch_shapes=[pltpu.VMEM((rank, tile), BF16), pltpu.VMEM((rank, virt), BF16)],
        ),
        compiler_params=params(54, dimension_semantics=("arbitrary",)),
        cost_estimate=pl.CostEstimate(
            flops=4 * virt * rank * (rank + virt) + 2 * virt**3,
            bytes_accessed=2 * rank * rank + 4 * virt * rank,
            transcendentals=0,
        ),
        name="ladder",
    )(slot, amps, ints, x, core, fock)


def half_kernel(slot, part_a, part_b, sum_ref, send_a, send_b, low_b, high_b):
    core = slot[0]
    send_a[...] = (part_a[...] - sum_ref[core].astype(F32)).astype(BF16)
    rounded = (part_b[...] - sum_ref[1 - core].astype(F32)).astype(BF16)
    send_b[...] = rounded

    @pl.when(pl.program_id(0) == 0)
    def _():
        low_b[...] = rounded

    @pl.when(pl.program_id(0) == 1)
    def _():
        high_b[...] = rounded


def half_of(slot, part_a, part_b, sums):
    virt = part_a.shape[0]
    rows = virt // 2
    strip = pl.BlockSpec((rows, virt), lambda r, s: (r, 0))
    return pl.pallas_call(
        half_kernel,
        out_shape=[jax.ShapeDtypeStruct((n, virt), BF16) for n in (virt, virt, rows, rows)],
        grid_spec=pltpu.PrefetchScalarGridSpec(
            num_scalar_prefetch=1,
            grid=(2,),
            in_specs=[strip, strip, pl.BlockSpec((2, rows, virt), lambda r, s: (0, r, 0))],
            out_specs=[strip, strip, whole((rows, virt)), whole((rows, virt))],
        ),
        compiler_params=params(16),
        cost_estimate=pl.CostEstimate(
            flops=0, bytes_accessed=16 * part_a.size, transcendentals=0
        ),
        name="half",
    )(slot, part_a, part_b, sums)


def finish_kernel(ids, part_a, part_b, sum_ref, amp_ref, col_ref, row_ref, occ_ref, *refs):
    near_a, far_a, same_a, low_b, near_b, far_b, same_b, res_ref, new_ref = refs
    step = pl.program_id(0)
    middle, diagonal = ids[5] == 1, ids[5] == 2

    def finish(part_ref, first, mirror):
        half = part_ref[...] - sum_ref[...].astype(F32)
        residual = half + mirror.astype(F32).T
        denominator = col_ref[...] + row_ref[...] - occ_ref[first] - occ_ref[ids[4]]
        res_ref[...] = residual
        new_ref[...] = (amp_ref[...].astype(F32) - residual / denominator).astype(BF16)

    @pl.when(step < 2)
    def _():
        mirror = jnp.where(middle, far_a[...], near_a[...])
        finish(part_a, ids[1], jnp.where(diagonal, same_a[...], mirror))

    @pl.when(step >= 2)
    def _():
        high = jnp.where(middle, far_b[...], near_b[...])
        mirror = jnp.concatenate([low_b[...], high], axis=0)
        finish(part_b, ids[3], jnp.where(diagonal, same_b[...], mirror))


def finish(ids, part_a, part_b, sums, amps, eps_col, eps_row, eps_occ, mirror_a, mirror_b):
    virt = part_a.shape[0]
    rows = virt // 2
    strip = pl.BlockSpec(
        (None, rows, virt), lambda g, s: (jnp.where(g < 2, s[0], s[2]), g % 2, 0)
    )

    def early(g, s):
        return jnp.minimum(g, 1)

    def late(g, s):
        return jnp.maximum(g - 2, 0)

    def across(m, at):
        return pl.BlockSpec((m.shape[0], rows), lambda g, s: (0, at(g, s)))

    return pl.pallas_call(
        finish_kernel,
        out_shape=[
            jax.ShapeDtypeStruct(amps.shape, F32),
            jax.ShapeDtypeStruct(amps.shape, BF16),
        ],
        grid_spec=pltpu.PrefetchScalarGridSpec(
            num_scalar_prefetch=1,
            grid=(4,),
            in_specs=[
                pl.BlockSpec((rows, virt), lambda g, s: (early(g, s), 0)),
                pl.BlockSpec((rows, virt), lambda g, s: (late(g, s), 0)),
                strip,
                strip,
                pl.BlockSpec((rows, 1), lambda g, s: (g % 2, 0)),
                whole((1, virt)),
                pl.BlockSpec(memory_space=pltpu.SMEM),
            ]
            + [across(m, early) for m in mirror_a]
            + [across(m, late) for m in mirror_b],
            out_specs=[strip, strip],
        ),
        compiler_params=params(24, dimension_semantics=("arbitrary",)),
        cost_estimate=pl.CostEstimate(
            flops=40 * part_a.size, bytes_accessed=28 * part_a.size, transcendentals=0
        ),
        name="finish",
    )(ids, part_a, part_b, sums, amps, eps_col, eps_row, eps_occ, *mirror_a, *mirror_b)


def shards(
    amplitudes,
    exch_int,
    thc_factor,
    thc_core,
    fock_vir,
    eps_vir,
    eps_occ,
    fock_occ,
    couple_list,
    couple_count,
):
    rows_i, _, virt, _ = amplitudes.shape
    n_first = lax.axis_size("occi")
    n_second = lax.axis_size("occj")
    me_i = lax.axis_index("occi")
    me_j = lax.axis_index("occj")
    core = me_j % 2
    slot_a = jnp.reshape(core, (1,)).astype(jnp.int32)
    slot_b = 1 - slot_a
    amps = amplitudes.reshape(rows_i, virt, virt)
    ints = exch_int.reshape(rows_i, virt, virt)

    size = n_first // 2

    def spot(y, low, x, high, c):
        return (2 * y + low) * n_second + 2 * (2 * x + high) + c

    def send(array, flip, diagonal=None, middle=None, other=None):
        pairs = []
        for y in range(size):
            for x in range(size):
                apart = (x - y) % size
                route = {0: diagonal, size // 2: middle}.get(apart, other)
                for low in range(2):
                    for high in range(2):
                        for c in range(2):
                            ends = dict(
                                mirror=((y, low, x, high), (x, high, y, low)),
                                inward=((y, low, x, high), (x, low, x, high)),
                                outward=((x, low, x, high), (x, high, y, low)),
                            ).get(route)
                            if ends:
                                pairs.append((spot(*ends[0], c), spot(*ends[1], c ^ flip)))
        return lax.ppermute(array, AXES, pairs)

    apart = (me_j // 4 - me_i // 2) % size
    kind = jnp.where(apart == size // 2, 1, jnp.where(apart == 0, 2, 0))
    eps_col = eps_vir.reshape(virt, 1)
    eps_row = eps_vir.reshape(1, virt)

    pair_ids = [slot_a[0], me_i * rows_i + slot_a[0], slot_b[0], me_i * rows_i + slot_b[0]]
    ids = jnp.stack([*pair_ids, me_j, kind]).astype(jnp.int32)

    slices = amps.reshape(n_second, rows_i * virt // n_second, virt)
    slices = lax.all_to_all(slices, "occj", 0, 0, tiled=True)
    weights = coupling(fock_occ, couple_list, couple_count)
    tall = jnp.repeat(jnp.repeat(weights, SUB, axis=0), SUB, axis=1)
    lane = jnp.arange(n_second * SUB, dtype=jnp.int32) % SUB
    wide = jnp.where(lane[:, None] == lane[None, :], tall, 0.0)
    part_a = ladder(slot_a, amps, ints, thc_factor, thc_core, fock_vir)
    slices, part_a, ids, eps_col = lax.optimization_barrier((slices, part_a, ids, eps_col))
    sums = mix(wide, slices)
    sums, part_a, slot_b = lax.optimization_barrier((sums, part_a, slot_b))
    sums = lax.all_to_all(sums, "occj", 0, 0, tiled=True)
    part_b = ladder(slot_b, amps, ints, thc_factor, thc_core, fock_vir)
    sums, part_b = lax.optimization_barrier((sums, part_b))
    sums = sums.reshape(rows_i, virt, virt)
    send_a, send_b, low_b, high_b = half_of(slot_a, part_a, part_b, sums)
    near_a = send(send_a, 0, middle="inward", other="mirror")
    near_b = send(high_b, 1, middle="inward", other="mirror")
    low_b = send(low_b, 1, middle="mirror", other="mirror")
    same_a = send(send_a, 0, diagonal="mirror")
    same_b = send(send_b, 1, diagonal="mirror")
    near_b, low_b = lax.optimization_barrier((near_b, low_b))
    far_a = send(near_a, 0, middle="outward")
    far_b = send(near_b, 0, middle="outward")
    mirror_a, mirror_b = (near_a, far_a, same_a), (low_b, near_b, far_b, same_b)
    residual, updated = finish(
        ids, part_a, part_b, sums, amps, eps_col, eps_row, eps_occ, mirror_a, mirror_b
    )
    return (
        residual.reshape(rows_i, 1, virt, virt),
        updated.reshape(rows_i, 1, virt, virt),
    )


def solution(mesh):
    pairs = P("occi", "occj", None, None)
    return jax.shard_map(
        shards,
        mesh=mesh,
        in_specs=(pairs, pairs) + (P(),) * 8,
        out_specs=(pairs, pairs),
        check_vma=False,
    )
```

```python
import functools

import jax
import jax.numpy as jnp
from jax import lax
from jax.experimental import pallas as pl
from jax.experimental.pallas import tpu as pltpu
from jax.sharding import PartitionSpec as P

AXES = ("occi", "occj")
F32 = jnp.float32
BF16 = jnp.bfloat16
SUB = 16


def coupling(fock_occ, couple_list, couple_count):
    n_occ = fock_occ.shape[0]
    slots = jnp.arange(couple_list.shape[1], dtype=jnp.int32)
    active = slots[None, :] < couple_count[:, None]
    target = jnp.arange(n_occ, dtype=jnp.int32)
    hits = (couple_list[:, :, None] == target[None, None, :]) & active[:, :, None]
    return fock_occ * jnp.sum(hits.astype(fock_occ.dtype), axis=1)


def params(limit, **kw):
    return pltpu.CompilerParams(vmem_limit_bytes=limit << 20, **kw)


def whole(shape):
    return pl.BlockSpec(shape, lambda *_: (0,) * len(shape))


def mix_kernel(w_ref, in_ref, out_ref):
    n = in_ref.shape[0]
    w = w_ref[...]
    high = w.astype(BF16)
    rest = w - high.astype(F32)
    mid = rest.astype(BF16)
    low = (rest - mid.astype(F32)).astype(BF16)
    for r in range(0, in_ref.shape[1], SUB):
        rhs = jnp.concatenate([in_ref[k, r : r + SUB, :] for k in range(n)], axis=0)
        total = jnp.dot(high, rhs, preferred_element_type=F32)
        total += jnp.dot(mid, rhs, preferred_element_type=F32)
        total += jnp.dot(low, rhs, preferred_element_type=F32)
        for j in range(n):
            out_ref[j, r : r + SUB, :] = total[j * SUB : (j + 1) * SUB, :].astype(BF16)


def mix(wide, slices):
    return pl.pallas_call(
        mix_kernel,
        out_shape=jax.ShapeDtypeStruct(slices.shape, BF16),
        grid=(1,),
        in_specs=[whole(wide.shape), whole(slices.shape)],
        out_specs=whole(slices.shape),
        compiler_params=params(16),
        cost_estimate=pl.CostEstimate(
            flops=10**9, bytes_accessed=4 * slices.size, transcendentals=0
        ),
        name="mix",
    )(wide, slices)


def ladder_kernel(slot, amp_ref, int_ref, x_ref, core_ref, fock_ref, out_ref, scaled, x_t):
    step = pl.program_id(0)
    tile = core_ref.shape[1]
    rank = x_ref.shape[1]
    chunk = min(512, rank)
    amp = amp_ref[...]

    @pl.when(step == 0)
    def _():
        for c in range(0, rank, min(256, rank)):
            cut = slice(c, c + min(256, rank))
            x_t[cut, :] = x_ref[:, cut].T
        virtual = jnp.dot(fock_ref[...], amp, preferred_element_type=F32)
        out_ref[...] = int_ref[...].astype(F32) + virtual

    cols = pl.ds(pl.multiple_of(step * tile, tile), tile)
    first = jnp.dot(amp, x_ref[:, cols], preferred_element_type=F32).astype(BF16)
    for p in range(0, rank, chunk):
        middle = jnp.dot(x_t[p : p + chunk, :], first, preferred_element_type=F32)
        scaled[p : p + chunk, :] = (core_ref[p : p + chunk, :].astype(F32) * middle).astype(BF16)
    second = jnp.dot(x_ref[...], scaled[...], preferred_element_type=F32).astype(BF16)
    out_ref[...] += jnp.dot(second, x_t[cols, :], preferred_element_type=F32)


def ladder(slot, amps, ints, x, core, fock):
    virt, rank = x.shape
    tile = min(512, rank)
    pair = pl.BlockSpec((None, virt, virt), lambda q, s: (s[0], 0, 0))
    return pl.pallas_call(
        ladder_kernel,
        out_shape=jax.ShapeDtypeStruct((virt, virt), F32),
        grid_spec=pltpu.PrefetchScalarGridSpec(
            num_scalar_prefetch=1,
            grid=(rank // tile,),
            in_specs=[
                pair,
                pair,
                whole(x.shape),
                pl.BlockSpec((rank, tile), lambda q, s: (0, q)),
                whole(fock.shape),
            ],
            out_specs=whole((virt, virt)),
            scratch_shapes=[pltpu.VMEM((rank, tile), BF16), pltpu.VMEM((rank, virt), BF16)],
        ),
        compiler_params=params(54, dimension_semantics=("arbitrary",)),
        cost_estimate=pl.CostEstimate(
            flops=4 * virt * rank * (rank + virt) + 2 * virt**3,
            bytes_accessed=2 * rank * rank + 4 * virt * rank,
            transcendentals=0,
        ),
        name="ladder",
    )(slot, amps, ints, x, core, fock)


def half_kernel(slot, part_a, part_b, sum_ref, send_a, send_b, low_b, high_b):
    core = slot[0]
    send_a[...] = (part_a[...] - sum_ref[core].astype(F32)).astype(BF16)
    rounded = (part_b[...] - sum_ref[1 - core].astype(F32)).astype(BF16)
    send_b[...] = rounded

    @pl.when(pl.program_id(0) == 0)
    def _():
        low_b[...] = rounded

    @pl.when(pl.program_id(0) == 1)
    def _():
        high_b[...] = rounded


def half_of(slot, part_a, part_b, sums):
    virt = part_a.shape[0]
    rows = virt // 2
    strip = pl.BlockSpec((rows, virt), lambda r, s: (r, 0))
    return pl.pallas_call(
        half_kernel,
        out_shape=[jax.ShapeDtypeStruct((n, virt), BF16) for n in (virt, virt, rows, rows)],
        grid_spec=pltpu.PrefetchScalarGridSpec(
            num_scalar_prefetch=1,
            grid=(2,),
            in_specs=[strip, strip, pl.BlockSpec((2, rows, virt), lambda r, s: (0, r, 0))],
            out_specs=[strip, strip, whole((rows, virt)), whole((rows, virt))],
        ),
        compiler_params=params(16),
        cost_estimate=pl.CostEstimate(
            flops=0, bytes_accessed=16 * part_a.size, transcendentals=0
        ),
        name="half",
    )(slot, part_a, part_b, sums)


def finish_kernel(split, ids, part_ref, sum_ref, amp_ref, col_ref, row_ref, occ_ref, *refs):
    res_ref, new_ref = refs[-2:]
    mirror = jnp.where(ids[3] == 1, refs[1][...], refs[0][...])
    if split:
        mirror = jnp.concatenate([refs[3][...], mirror], axis=0)
    mirror = jnp.where(ids[3] == 2, refs[2][...], mirror)
    half = part_ref[...] - sum_ref[...].astype(F32)
    residual = half + mirror.astype(F32).T
    denominator = col_ref[...] + row_ref[...] - occ_ref[ids[1]] - occ_ref[ids[2]]
    res_ref[...] = residual
    new_ref[...] = (amp_ref[...].astype(F32) - residual / denominator).astype(BF16)


def finish(ids, part, sums, mirrors, amps, eps_col, eps_row, eps_occ, held):
    virt = part.shape[0]
    rows = min(256, virt)
    strip = pl.BlockSpec((None, rows, virt), lambda r, s: (s[0], r, 0))
    return pl.pallas_call(
        functools.partial(finish_kernel, len(mirrors) > 3),
        out_shape=[
            jax.ShapeDtypeStruct(amps.shape, F32),
            jax.ShapeDtypeStruct(amps.shape, BF16),
        ],
        grid_spec=pltpu.PrefetchScalarGridSpec(
            num_scalar_prefetch=1,
            grid=(virt // rows,),
            in_specs=[
                pl.BlockSpec((rows, virt), lambda r, s: (r, 0)),
                strip,
                strip,
                pl.BlockSpec((rows, 1), lambda r, s: (r, 0)),
                whole((1, virt)),
                pl.BlockSpec(memory_space=pltpu.SMEM),
            ]
            + [pl.BlockSpec((m.shape[0], rows), lambda r, s: (0, r)) for m in mirrors]
            + [pl.BlockSpec(memory_space=pl.ANY)] * len(held),
            out_specs=[strip, strip],
        ),
        input_output_aliases={7 + len(mirrors) + m: m for m in range(len(held))},
        compiler_params=params(16, dimension_semantics=("arbitrary",)),
        cost_estimate=pl.CostEstimate(
            flops=20 * part.size, bytes_accessed=14 * part.size, transcendentals=0
        ),
        name="finish",
    )(ids, part, sums, amps, eps_col, eps_row, eps_occ, *mirrors, *held)


def shards(
    amplitudes,
    exch_int,
    thc_factor,
    thc_core,
    fock_vir,
    eps_vir,
    eps_occ,
    fock_occ,
    couple_list,
    couple_count,
):
    rows_i, _, virt, _ = amplitudes.shape
    n_first = lax.axis_size("occi")
    n_second = lax.axis_size("occj")
    me_i = lax.axis_index("occi")
    me_j = lax.axis_index("occj")
    core = me_j % 2
    slot_a = jnp.reshape(core, (1,)).astype(jnp.int32)
    slot_b = 1 - slot_a
    amps = amplitudes.reshape(rows_i, virt, virt)
    ints = exch_int.reshape(rows_i, virt, virt)

    size = n_first // 2

    def spot(y, low, x, high, c):
        return (2 * y + low) * n_second + 2 * (2 * x + high) + c

    def send(array, flip, diagonal=None, middle=None, other=None):
        pairs = []
        for y in range(size):
            for x in range(size):
                apart = (x - y) % size
                route = {0: diagonal, size // 2: middle}.get(apart, other)
                for low in range(2):
                    for high in range(2):
                        for c in range(2):
                            ends = dict(
                                mirror=((y, low, x, high), (x, high, y, low)),
                                inward=((y, low, x, high), (x, low, x, high)),
                                outward=((x, low, x, high), (x, high, y, low)),
                            ).get(route)
                            if ends:
                                pairs.append((spot(*ends[0], c), spot(*ends[1], c ^ flip)))
        return lax.ppermute(array, AXES, pairs)

    apart = (me_j // 4 - me_i // 2) % size
    kind = jnp.where(apart == size // 2, 1, jnp.where(apart == 0, 2, 0))
    eps_col = eps_vir.reshape(virt, 1)
    eps_row = eps_vir.reshape(1, virt)

    def ids_of(slot):
        return jnp.stack([slot[0], me_i * rows_i + slot[0], me_j, kind]).astype(jnp.int32)

    ids_a, ids_b = ids_of(slot_a), ids_of(slot_b)

    slices = amps.reshape(n_second, rows_i * virt // n_second, virt)
    slices = lax.all_to_all(slices, "occj", 0, 0, tiled=True)
    weights = coupling(fock_occ, couple_list, couple_count)
    tall = jnp.repeat(jnp.repeat(weights, SUB, axis=0), SUB, axis=1)
    lane = jnp.arange(n_second * SUB, dtype=jnp.int32) % SUB
    wide = jnp.where(lane[:, None] == lane[None, :], tall, 0.0)
    part_a = ladder(slot_a, amps, ints, thc_factor, thc_core, fock_vir)
    slices, part_a, ids_a, ids_b, eps_col = lax.optimization_barrier(
        (slices, part_a, ids_a, ids_b, eps_col)
    )
    sums = mix(wide, slices)
    sums, part_a, slot_b = lax.optimization_barrier((sums, part_a, slot_b))
    sums = lax.all_to_all(sums, "occj", 0, 0, tiled=True)
    part_b = ladder(slot_b, amps, ints, thc_factor, thc_core, fock_vir)
    sums, part_b = lax.optimization_barrier((sums, part_b))
    sums = sums.reshape(rows_i, virt, virt)
    send_a, send_b, low_b, high_b = half_of(slot_a, part_a, part_b, sums)
    near_a = send(send_a, 0, middle="inward", other="mirror")
    low_b = send(low_b, 1, middle="mirror", other="mirror")
    near_b = send(high_b, 1, middle="inward", other="mirror")
    same_a = send(send_a, 0, diagonal="mirror")
    same_b = send(send_b, 1, diagonal="mirror")
    low_b, near_b = lax.optimization_barrier((low_b, near_b))
    far_a = send(near_a, 0, middle="outward")
    far_b = send(near_b, 0, middle="outward")

    far_a, far_b = lax.optimization_barrier((far_a, far_b))
    tables = (amps, eps_col, eps_row, eps_occ)
    mirror_a = (near_a, far_a, same_a)
    mirror_b = (near_b, far_b, same_b, low_b)
    held = finish(ids_a, part_a, sums, mirror_a, *tables, ())
    residual, updated = finish(ids_b, part_b, sums, mirror_b, *tables, held)
    return (
        residual.reshape(rows_i, 1, virt, virt),
        updated.reshape(rows_i, 1, virt, virt),
    )


def solution(mesh):
    pairs = P("occi", "occj", None, None)
    return jax.shard_map(
        shards,
        mesh=mesh,
        in_specs=(pairs, pairs) + (P(),) * 8,
        out_specs=(pairs, pairs),
        check_vma=False,
    )
```

```python
import functools

import jax
import jax.numpy as jnp
from jax import lax
from jax.experimental import pallas as pl
from jax.experimental.pallas import tpu as pltpu
from jax.sharding import PartitionSpec as P

AXES = ("occi", "occj")
F32 = jnp.float32
BF16 = jnp.bfloat16
SUB = 16


def coupling(fock_occ, couple_list, couple_count):
    n_occ = fock_occ.shape[0]
    slots = jnp.arange(couple_list.shape[1], dtype=jnp.int32)
    active = slots[None, :] < couple_count[:, None]
    target = jnp.arange(n_occ, dtype=jnp.int32)
    hits = (couple_list[:, :, None] == target[None, None, :]) & active[:, :, None]
    return fock_occ * jnp.sum(hits.astype(fock_occ.dtype), axis=1)


def params(limit, **kw):
    return pltpu.CompilerParams(vmem_limit_bytes=limit << 20, **kw)


def whole(shape):
    return pl.BlockSpec(shape, lambda *_: (0,) * len(shape))


def mix_kernel(w_ref, in_ref, out_ref):
    n = in_ref.shape[0]
    w = w_ref[...]
    high = w.astype(BF16)
    rest = w - high.astype(F32)
    mid = rest.astype(BF16)
    low = (rest - mid.astype(F32)).astype(BF16)
    for r in range(0, in_ref.shape[1], SUB):
        rhs = jnp.concatenate([in_ref[k, r : r + SUB, :] for k in range(n)], axis=0)
        total = jnp.dot(high, rhs, preferred_element_type=F32)
        total += jnp.dot(mid, rhs, preferred_element_type=F32)
        total += jnp.dot(low, rhs, preferred_element_type=F32)
        for j in range(n):
            out_ref[j, r : r + SUB, :] = total[j * SUB : (j + 1) * SUB, :].astype(BF16)


def mix(wide, slices):
    return pl.pallas_call(
        mix_kernel,
        out_shape=jax.ShapeDtypeStruct(slices.shape, BF16),
        grid=(1,),
        in_specs=[whole(wide.shape), whole(slices.shape)],
        out_specs=whole(slices.shape),
        compiler_params=params(16),
        cost_estimate=pl.CostEstimate(
            flops=10**9, bytes_accessed=4 * slices.size, transcendentals=0
        ),
        name="mix",
    )(wide, slices)


def ladder_kernel(slot, amp_ref, int_ref, x_ref, core_ref, fock_ref, out_ref, scaled, x_t):
    step = pl.program_id(0)
    tile = core_ref.shape[1]
    rank = x_ref.shape[1]
    chunk = min(512, rank)
    amp = amp_ref[...]

    @pl.when(step == 0)
    def _():
        for c in range(0, rank, min(256, rank)):
            cut = slice(c, c + min(256, rank))
            x_t[cut, :] = x_ref[:, cut].T
        virtual = jnp.dot(fock_ref[...], amp, preferred_element_type=F32)
        out_ref[...] = int_ref[...].astype(F32) + virtual

    cols = pl.ds(pl.multiple_of(step * tile, tile), tile)
    first = jnp.dot(amp, x_ref[:, cols], preferred_element_type=F32).astype(BF16)
    for p in range(0, rank, chunk):
        middle = jnp.dot(x_t[p : p + chunk, :], first, preferred_element_type=F32)
        scaled[p : p + chunk, :] = (core_ref[p : p + chunk, :].astype(F32) * middle).astype(BF16)
    second = jnp.dot(x_ref[...], scaled[...], preferred_element_type=F32).astype(BF16)
    out_ref[...] += jnp.dot(second, x_t[cols, :], preferred_element_type=F32)


def ladder(slot, amps, ints, x, core, fock):
    virt, rank = x.shape
    tile = min(512, rank)
    pair = pl.BlockSpec((None, virt, virt), lambda q, s: (s[0], 0, 0))
    return pl.pallas_call(
        ladder_kernel,
        out_shape=jax.ShapeDtypeStruct((virt, virt), F32),
        grid_spec=pltpu.PrefetchScalarGridSpec(
            num_scalar_prefetch=1,
            grid=(rank // tile,),
            in_specs=[
                pair,
                pair,
                whole(x.shape),
                pl.BlockSpec((rank, tile), lambda q, s: (0, q)),
                whole(fock.shape),
            ],
            out_specs=whole((virt, virt)),
            scratch_shapes=[pltpu.VMEM((rank, tile), BF16), pltpu.VMEM((rank, virt), BF16)],
        ),
        compiler_params=params(54, dimension_semantics=("arbitrary",)),
        cost_estimate=pl.CostEstimate(
            flops=4 * virt * rank * (rank + virt) + 2 * virt**3,
            bytes_accessed=2 * rank * rank + 4 * virt * rank,
            transcendentals=0,
        ),
        name="ladder",
    )(slot, amps, ints, x, core, fock)


def half_kernel(slot, part_a, part_b, sum_ref, send_a, send_b, low_b, high_b):
    core = slot[0]
    send_a[...] = (part_a[...] - sum_ref[core].astype(F32)).astype(BF16)
    rounded = (part_b[...] - sum_ref[1 - core].astype(F32)).astype(BF16)
    send_b[...] = rounded

    @pl.when(pl.program_id(0) == 0)
    def _():
        low_b[...] = rounded

    @pl.when(pl.program_id(0) == 1)
    def _():
        high_b[...] = rounded


def half_of(slot, part_a, part_b, sums):
    virt = part_a.shape[0]
    rows = virt // 2
    strip = pl.BlockSpec((rows, virt), lambda r, s: (r, 0))
    return pl.pallas_call(
        half_kernel,
        out_shape=[jax.ShapeDtypeStruct((n, virt), BF16) for n in (virt, virt, rows, rows)],
        grid_spec=pltpu.PrefetchScalarGridSpec(
            num_scalar_prefetch=1,
            grid=(2,),
            in_specs=[strip, strip, pl.BlockSpec((2, rows, virt), lambda r, s: (0, r, 0))],
            out_specs=[strip, strip, whole((rows, virt)), whole((rows, virt))],
        ),
        compiler_params=params(16),
        cost_estimate=pl.CostEstimate(
            flops=0, bytes_accessed=16 * part_a.size, transcendentals=0
        ),
        name="half",
    )(slot, part_a, part_b, sums)


def finish_kernel(ids, part_a, part_b, sum_ref, amp_ref, col_ref, row_ref, occ_ref, *refs):
    near_a, far_a, same_a, low_b, near_b, far_b, same_b, res_ref, new_ref = refs
    step = pl.program_id(0)
    middle, diagonal = ids[5] == 1, ids[5] == 2

    def finish(part_ref, first, mirror):
        half = part_ref[...] - sum_ref[...].astype(F32)
        residual = half + mirror.astype(F32).T
        denominator = col_ref[...] + row_ref[...] - occ_ref[first] - occ_ref[ids[4]]
        res_ref[...] = residual
        new_ref[...] = (amp_ref[...].astype(F32) - residual / denominator).astype(BF16)

    @pl.when(step < 2)
    def _():
        mirror = jnp.where(middle, far_a[...], near_a[...])
        finish(part_a, ids[1], jnp.where(diagonal, same_a[...], mirror))

    @pl.when(step >= 2)
    def _():
        high = jnp.where(middle, far_b[...], near_b[...])
        mirror = jnp.concatenate([low_b[...], high], axis=0)
        finish(part_b, ids[3], jnp.where(diagonal, same_b[...], mirror))


def finish(ids, part_a, part_b, sums, amps, eps_col, eps_row, eps_occ, mirror_a, mirror_b):
    virt = part_a.shape[0]
    rows = virt // 2
    strip = pl.BlockSpec(
        (None, rows, virt), lambda g, s: (jnp.where(g < 2, s[0], s[2]), g % 2, 0)
    )

    def early(g, s):
        return jnp.minimum(g, 1)

    def late(g, s):
        return jnp.maximum(g - 2, 0)

    def across(m, at):
        return pl.BlockSpec((m.shape[0], rows), lambda g, s: (0, at(g, s)))

    return pl.pallas_call(
        finish_kernel,
        out_shape=[
            jax.ShapeDtypeStruct(amps.shape, F32),
            jax.ShapeDtypeStruct(amps.shape, BF16),
        ],
        grid_spec=pltpu.PrefetchScalarGridSpec(
            num_scalar_prefetch=1,
            grid=(4,),
            in_specs=[
                pl.BlockSpec((rows, virt), lambda g, s: (early(g, s), 0)),
                pl.BlockSpec((rows, virt), lambda g, s: (late(g, s), 0)),
                strip,
                strip,
                pl.BlockSpec((rows, 1), lambda g, s: (g % 2, 0)),
                whole((1, virt)),
                pl.BlockSpec(memory_space=pltpu.SMEM),
            ]
            + [across(m, early) for m in mirror_a]
            + [across(m, late) for m in mirror_b],
            out_specs=[strip, strip],
        ),
        compiler_params=params(52, dimension_semantics=("arbitrary",)),
        cost_estimate=pl.CostEstimate(
            flops=40 * part_a.size, bytes_accessed=28 * part_a.size, transcendentals=0
        ),
        name="finish",
    )(ids, part_a, part_b, sums, amps, eps_col, eps_row, eps_occ, *mirror_a, *mirror_b)


def shards(
    amplitudes,
    exch_int,
    thc_factor,
    thc_core,
    fock_vir,
    eps_vir,
    eps_occ,
    fock_occ,
    couple_list,
    couple_count,
):
    rows_i, _, virt, _ = amplitudes.shape
    n_first = lax.axis_size("occi")
    n_second = lax.axis_size("occj")
    me_i = lax.axis_index("occi")
    me_j = lax.axis_index("occj")
    core = me_j % 2
    slot_a = jnp.reshape(core, (1,)).astype(jnp.int32)
    slot_b = 1 - slot_a
    amps = amplitudes.reshape(rows_i, virt, virt)
    ints = exch_int.reshape(rows_i, virt, virt)

    size = n_first // 2

    def spot(y, low, x, high, c):
        return (2 * y + low) * n_second + 2 * (2 * x + high) + c

    def send(array, flip, diagonal=None, middle=None, other=None):
        pairs = []
        for y in range(size):
            for x in range(size):
                apart = (x - y) % size
                route = {0: diagonal, size // 2: middle}.get(apart, other)
                for low in range(2):
                    for high in range(2):
                        for c in range(2):
                            ends = dict(
                                mirror=((y, low, x, high), (x, high, y, low)),
                                inward=((y, low, x, high), (x, low, x, high)),
                                outward=((x, low, x, high), (x, high, y, low)),
                            ).get(route)
                            if ends:
                                pairs.append((spot(*ends[0], c), spot(*ends[1], c ^ flip)))
        return lax.ppermute(array, AXES, pairs)

    apart = (me_j // 4 - me_i // 2) % size
    kind = jnp.where(apart == size // 2, 1, jnp.where(apart == 0, 2, 0))
    eps_col = eps_vir.reshape(virt, 1)
    eps_row = eps_vir.reshape(1, virt)

    pair_ids = [slot_a[0], me_i * rows_i + slot_a[0], slot_b[0], me_i * rows_i + slot_b[0]]
    ids = jnp.stack([*pair_ids, me_j, kind]).astype(jnp.int32)

    slices = amps.reshape(n_second, rows_i * virt // n_second, virt)
    slices = lax.all_to_all(slices, "occj", 0, 0, tiled=True)
    weights = coupling(fock_occ, couple_list, couple_count)
    tall = jnp.repeat(jnp.repeat(weights, SUB, axis=0), SUB, axis=1)
    lane = jnp.arange(n_second * SUB, dtype=jnp.int32) % SUB
    wide = jnp.where(lane[:, None] == lane[None, :], tall, 0.0)
    part_a = ladder(slot_a, amps, ints, thc_factor, thc_core, fock_vir)
    slices, part_a, ids, eps_col = lax.optimization_barrier((slices, part_a, ids, eps_col))
    sums = mix(wide, slices)
    sums, part_a, slot_b = lax.optimization_barrier((sums, part_a, slot_b))
    sums = lax.all_to_all(sums, "occj", 0, 0, tiled=True)
    part_b = ladder(slot_b, amps, ints, thc_factor, thc_core, fock_vir)
    sums, part_b = lax.optimization_barrier((sums, part_b))
    sums = sums.reshape(rows_i, virt, virt)
    send_a, send_b, low_b, high_b = half_of(slot_a, part_a, part_b, sums)
    near_a = send(send_a, 0, middle="inward", other="mirror")
    low_b = send(low_b, 1, middle="mirror", other="mirror")
    near_b = send(high_b, 1, middle="inward", other="mirror")
    same_a = send(send_a, 0, diagonal="mirror")
    same_b = send(send_b, 1, diagonal="mirror")
    low_b, near_b = lax.optimization_barrier((low_b, near_b))
    far_a = send(near_a, 0, middle="outward")
    far_b = send(near_b, 0, middle="outward")
    mirror_a, mirror_b = (near_a, far_a, same_a), (low_b, near_b, far_b, same_b)
    residual, updated = finish(
        ids, part_a, part_b, sums, amps, eps_col, eps_row, eps_occ, mirror_a, mirror_b
    )
    return (
        residual.reshape(rows_i, 1, virt, virt),
        updated.reshape(rows_i, 1, virt, virt),
    )


def solution(mesh):
    pairs = P("occi", "occj", None, None)
    return jax.shard_map(
        shards,
        mesh=mesh,
        in_specs=(pairs, pairs) + (P(),) * 8,
        out_specs=(pairs, pairs),
        check_vma=False,
    )
```

```python
import functools

import jax
import jax.numpy as jnp
from jax import lax
from jax.experimental import pallas as pl
from jax.experimental.pallas import tpu as pltpu
from jax.sharding import PartitionSpec as P

AXES = ("occi", "occj")
F32 = jnp.float32
BF16 = jnp.bfloat16
SUB = 16


def coupling(fock_occ, couple_list, couple_count):
    n_occ = fock_occ.shape[0]
    slots = jnp.arange(couple_list.shape[1], dtype=jnp.int32)
    active = slots[None, :] < couple_count[:, None]
    target = jnp.arange(n_occ, dtype=jnp.int32)
    hits = (couple_list[:, :, None] == target[None, None, :]) & active[:, :, None]
    return fock_occ * jnp.sum(hits.astype(fock_occ.dtype), axis=1)


def params(limit, **kw):
    return pltpu.CompilerParams(vmem_limit_bytes=limit << 20, **kw)


def whole(shape):
    return pl.BlockSpec(shape, lambda *_: (0,) * len(shape))


def mix_kernel(w_ref, in_ref, out_ref):
    n = in_ref.shape[0]
    w = w_ref[...]
    high = w.astype(BF16)
    rest = w - high.astype(F32)
    mid = rest.astype(BF16)
    low = (rest - mid.astype(F32)).astype(BF16)
    for r in range(0, in_ref.shape[1], SUB):
        rhs = jnp.concatenate([in_ref[k, r : r + SUB, :] for k in range(n)], axis=0)
        total = jnp.dot(high, rhs, preferred_element_type=F32)
        total += jnp.dot(mid, rhs, preferred_element_type=F32)
        total += jnp.dot(low, rhs, preferred_element_type=F32)
        for j in range(n):
            out_ref[j, r : r + SUB, :] = total[j * SUB : (j + 1) * SUB, :].astype(BF16)


def mix(wide, slices):
    return pl.pallas_call(
        mix_kernel,
        out_shape=jax.ShapeDtypeStruct(slices.shape, BF16),
        grid=(1,),
        in_specs=[whole(wide.shape), whole(slices.shape)],
        out_specs=whole(slices.shape),
        compiler_params=params(16),
        cost_estimate=pl.CostEstimate(
            flops=10**9, bytes_accessed=4 * slices.size, transcendentals=0
        ),
        name="mix",
    )(wide, slices)


def ladder_kernel(slot, amp_ref, int_ref, x_ref, core_ref, fock_ref, out_ref, scaled, x_t):
    step = pl.program_id(0)
    tile = core_ref.shape[1]
    rank = x_ref.shape[1]
    chunk = min(512, rank)
    amp = amp_ref[...]

    @pl.when(step == 0)
    def _():
        for c in range(0, rank, min(256, rank)):
            cut = slice(c, c + min(256, rank))
            x_t[cut, :] = x_ref[:, cut].T
        virtual = jnp.dot(fock_ref[...], amp, preferred_element_type=F32)
        out_ref[...] = int_ref[...].astype(F32) + virtual

    cols = pl.ds(pl.multiple_of(step * tile, tile), tile)
    first = jnp.dot(amp, x_ref[:, cols], preferred_element_type=F32).astype(BF16)
    for p in range(0, rank, chunk):
        middle = jnp.dot(x_t[p : p + chunk, :], first, preferred_element_type=F32)
        scaled[p : p + chunk, :] = (core_ref[p : p + chunk, :].astype(F32) * middle).astype(BF16)
    second = jnp.dot(x_ref[...], scaled[...], preferred_element_type=F32).astype(BF16)
    out_ref[...] += jnp.dot(second, x_t[cols, :], preferred_element_type=F32)


def ladder(slot, amps, ints, x, core, fock):
    virt, rank = x.shape
    tile = min(512, rank)
    pair = pl.BlockSpec((None, virt, virt), lambda q, s: (s[0], 0, 0))
    return pl.pallas_call(
        ladder_kernel,
        out_shape=jax.ShapeDtypeStruct((virt, virt), F32),
        grid_spec=pltpu.PrefetchScalarGridSpec(
            num_scalar_prefetch=1,
            grid=(rank // tile,),
            in_specs=[
                pair,
                pair,
                whole(x.shape),
                pl.BlockSpec((rank, tile), lambda q, s: (0, q)),
                whole(fock.shape),
            ],
            out_specs=whole((virt, virt)),
            scratch_shapes=[pltpu.VMEM((rank, tile), BF16), pltpu.VMEM((rank, virt), BF16)],
        ),
        compiler_params=params(54, dimension_semantics=("arbitrary",)),
        cost_estimate=pl.CostEstimate(
            flops=4 * virt * rank * (rank + virt) + 2 * virt**3,
            bytes_accessed=2 * rank * rank + 4 * virt * rank,
            transcendentals=0,
        ),
        name="ladder",
    )(slot, amps, ints, x, core, fock)


def half_kernel(slot, part_a, part_b, sum_ref, send_a, send_b, low_b, high_b):
    core = slot[0]
    send_a[...] = (part_a[...] - sum_ref[core].astype(F32)).astype(BF16)
    rounded = (part_b[...] - sum_ref[1 - core].astype(F32)).astype(BF16)
    send_b[...] = rounded

    @pl.when(pl.program_id(0) == 0)
    def _():
        low_b[...] = rounded

    @pl.when(pl.program_id(0) == 1)
    def _():
        high_b[...] = rounded


def half_of(slot, part_a, part_b, sums):
    virt = part_a.shape[0]
    rows = virt // 2
    strip = pl.BlockSpec((rows, virt), lambda r, s: (r, 0))
    return pl.pallas_call(
        half_kernel,
        out_shape=[jax.ShapeDtypeStruct((n, virt), BF16) for n in (virt, virt, rows, rows)],
        grid_spec=pltpu.PrefetchScalarGridSpec(
            num_scalar_prefetch=1,
            grid=(2,),
            in_specs=[strip, strip, pl.BlockSpec((2, rows, virt), lambda r, s: (0, r, 0))],
            out_specs=[strip, strip, whole((rows, virt)), whole((rows, virt))],
        ),
        compiler_params=params(16),
        cost_estimate=pl.CostEstimate(
            flops=0, bytes_accessed=16 * part_a.size, transcendentals=0
        ),
        name="half",
    )(slot, part_a, part_b, sums)


def finish_kernel(ids, part_a, part_b, sum_ref, amp_ref, col_ref, row_ref, occ_ref, *refs):
    near_a, far_a, same_a, low_b, near_b, far_b, same_b, res_ref, new_ref = refs
    step = pl.program_id(0)
    middle, diagonal = ids[5] == 1, ids[5] == 2

    def finish(part_ref, first, mirror):
        half = part_ref[...] - sum_ref[...].astype(F32)
        residual = half + mirror.T.astype(F32)
        denominator = col_ref[...] + row_ref[...] - occ_ref[first] - occ_ref[ids[4]]
        res_ref[...] = residual
        new_ref[...] = (amp_ref[...].astype(F32) - residual / denominator).astype(BF16)

    @pl.when(step < 2)
    def _():
        mirror = jnp.where(middle, far_a[...], near_a[...])
        finish(part_a, ids[1], jnp.where(diagonal, same_a[...], mirror))

    @pl.when(step >= 2)
    def _():
        high = jnp.where(middle, far_b[...], near_b[...])
        mirror = jnp.concatenate([low_b[...], high], axis=0)
        finish(part_b, ids[3], jnp.where(diagonal, same_b[...], mirror))


def finish(ids, part_a, part_b, sums, amps, eps_col, eps_row, eps_occ, mirror_a, mirror_b):
    virt = part_a.shape[0]
    rows = virt // 2
    strip = pl.BlockSpec(
        (None, rows, virt), lambda g, s: (jnp.where(g < 2, s[0], s[2]), g % 2, 0)
    )

    def early(g, s):
        return jnp.minimum(g, 1)

    def late(g, s):
        return jnp.maximum(g - 2, 0)

    def across(m, at):
        return pl.BlockSpec((m.shape[0], rows), lambda g, s: (0, at(g, s)))

    return pl.pallas_call(
        finish_kernel,
        out_shape=[
            jax.ShapeDtypeStruct(amps.shape, F32),
            jax.ShapeDtypeStruct(amps.shape, BF16),
        ],
        grid_spec=pltpu.PrefetchScalarGridSpec(
            num_scalar_prefetch=1,
            grid=(4,),
            in_specs=[
                pl.BlockSpec((rows, virt), lambda g, s: (early(g, s), 0)),
                pl.BlockSpec((rows, virt), lambda g, s: (late(g, s), 0)),
                strip,
                strip,
                pl.BlockSpec((rows, 1), lambda g, s: (g % 2, 0)),
                whole((1, virt)),
                pl.BlockSpec(memory_space=pltpu.SMEM),
            ]
            + [across(m, early) for m in mirror_a]
            + [across(m, late) for m in mirror_b],
            out_specs=[strip, strip],
        ),
        compiler_params=params(52, dimension_semantics=("arbitrary",)),
        cost_estimate=pl.CostEstimate(
            flops=40 * part_a.size, bytes_accessed=28 * part_a.size, transcendentals=0
        ),
        name="finish",
    )(ids, part_a, part_b, sums, amps, eps_col, eps_row, eps_occ, *mirror_a, *mirror_b)


def shards(
    amplitudes,
    exch_int,
    thc_factor,
    thc_core,
    fock_vir,
    eps_vir,
    eps_occ,
    fock_occ,
    couple_list,
    couple_count,
):
    rows_i, _, virt, _ = amplitudes.shape
    n_first = lax.axis_size("occi")
    n_second = lax.axis_size("occj")
    me_i = lax.axis_index("occi")
    me_j = lax.axis_index("occj")
    core = me_j % 2
    slot_a = jnp.reshape(core, (1,)).astype(jnp.int32)
    slot_b = 1 - slot_a
    amps = amplitudes.reshape(rows_i, virt, virt)
    ints = exch_int.reshape(rows_i, virt, virt)

    size = n_first // 2

    def spot(y, low, x, high, c):
        return (2 * y + low) * n_second + 2 * (2 * x + high) + c

    def send(array, flip, diagonal=None, middle=None, other=None):
        pairs = []
        for y in range(size):
            for x in range(size):
                apart = (x - y) % size
                route = {0: diagonal, size // 2: middle}.get(apart, other)
                for low in range(2):
                    for high in range(2):
                        for c in range(2):
                            ends = dict(
                                mirror=((y, low, x, high), (x, high, y, low)),
                                inward=((y, low, x, high), (x, low, x, high)),
                                outward=((x, low, x, high), (x, high, y, low)),
                            ).get(route)
                            if ends:
                                pairs.append((spot(*ends[0], c), spot(*ends[1], c ^ flip)))
        return lax.ppermute(array, AXES, pairs)

    apart = (me_j // 4 - me_i // 2) % size
    kind = jnp.where(apart == size // 2, 1, jnp.where(apart == 0, 2, 0))
    eps_col = eps_vir.reshape(virt, 1)
    eps_row = eps_vir.reshape(1, virt)

    pair_ids = [slot_a[0], me_i * rows_i + slot_a[0], slot_b[0], me_i * rows_i + slot_b[0]]
    ids = jnp.stack([*pair_ids, me_j, kind]).astype(jnp.int32)

    slices = amps.reshape(n_second, rows_i * virt // n_second, virt)
    slices = lax.all_to_all(slices, "occj", 0, 0, tiled=True)
    weights = coupling(fock_occ, couple_list, couple_count)
    tall = jnp.repeat(jnp.repeat(weights, SUB, axis=0), SUB, axis=1)
    lane = jnp.arange(n_second * SUB, dtype=jnp.int32) % SUB
    wide = jnp.where(lane[:, None] == lane[None, :], tall, 0.0)
    part_a = ladder(slot_a, amps, ints, thc_factor, thc_core, fock_vir)
    slices, part_a, ids, eps_col = lax.optimization_barrier((slices, part_a, ids, eps_col))
    sums = mix(wide, slices)
    sums, part_a, slot_b = lax.optimization_barrier((sums, part_a, slot_b))
    sums = lax.all_to_all(sums, "occj", 0, 0, tiled=True)
    part_b = ladder(slot_b, amps, ints, thc_factor, thc_core, fock_vir)
    sums, part_b = lax.optimization_barrier((sums, part_b))
    sums = sums.reshape(rows_i, virt, virt)
    send_a, send_b, low_b, high_b = half_of(slot_a, part_a, part_b, sums)
    near_a = send(send_a, 0, middle="inward", other="mirror")
    low_b = send(low_b, 1, middle="mirror", other="mirror")
    near_b = send(high_b, 1, middle="inward", other="mirror")
    same_a = send(send_a, 0, diagonal="mirror")
    same_b = send(send_b, 1, diagonal="mirror")
    low_b, near_b = lax.optimization_barrier((low_b, near_b))
    far_a = send(near_a, 0, middle="outward")
    far_b = send(near_b, 0, middle="outward")
    mirror_a, mirror_b = (near_a, far_a, same_a), (low_b, near_b, far_b, same_b)
    residual, updated = finish(
        ids, part_a, part_b, sums, amps, eps_col, eps_row, eps_occ, mirror_a, mirror_b
    )
    return (
        residual.reshape(rows_i, 1, virt, virt),
        updated.reshape(rows_i, 1, virt, virt),
    )


def solution(mesh):
    pairs = P("occi", "occj", None, None)
    return jax.shard_map(
        shards,
        mesh=mesh,
        in_specs=(pairs, pairs) + (P(),) * 8,
        out_specs=(pairs, pairs),
        check_vma=False,
    )
```

```python
import functools

import jax
import jax.numpy as jnp
from jax import lax
from jax.experimental import pallas as pl
from jax.experimental.pallas import tpu as pltpu
from jax.sharding import PartitionSpec as P

AXES = ("occi", "occj")
F32 = jnp.float32
BF16 = jnp.bfloat16
SUB = 16


def coupling(fock_occ, couple_list, couple_count):
    n_occ = fock_occ.shape[0]
    slots = jnp.arange(couple_list.shape[1], dtype=jnp.int32)
    active = slots[None, :] < couple_count[:, None]
    target = jnp.arange(n_occ, dtype=jnp.int32)
    hits = (couple_list[:, :, None] == target[None, None, :]) & active[:, :, None]
    return fock_occ * jnp.sum(hits.astype(fock_occ.dtype), axis=1)


def params(limit, **kw):
    return pltpu.CompilerParams(vmem_limit_bytes=limit << 20, **kw)


def whole(shape):
    return pl.BlockSpec(shape, lambda *_: (0,) * len(shape))


def mix_kernel(w_ref, in_ref, out_ref):
    n = in_ref.shape[0]
    w = w_ref[...]
    high = w.astype(BF16)
    rest = w - high.astype(F32)
    mid = rest.astype(BF16)
    low = (rest - mid.astype(F32)).astype(BF16)
    for r in range(0, in_ref.shape[1], SUB):
        rhs = jnp.concatenate([in_ref[k, r : r + SUB, :] for k in range(n)], axis=0)
        total = jnp.dot(high, rhs, preferred_element_type=F32)
        total += jnp.dot(mid, rhs, preferred_element_type=F32)
        total += jnp.dot(low, rhs, preferred_element_type=F32)
        for j in range(n):
            out_ref[j, r : r + SUB, :] = total[j * SUB : (j + 1) * SUB, :].astype(BF16)


def mix(wide, slices):
    return pl.pallas_call(
        mix_kernel,
        out_shape=jax.ShapeDtypeStruct(slices.shape, BF16),
        grid=(1,),
        in_specs=[whole(wide.shape), whole(slices.shape)],
        out_specs=whole(slices.shape),
        compiler_params=params(16),
        cost_estimate=pl.CostEstimate(
            flops=10**9, bytes_accessed=4 * slices.size, transcendentals=0
        ),
        name="mix",
    )(wide, slices)


def ladder_kernel(slot, amp_ref, int_ref, x_ref, core_ref, fock_ref, out_ref, scaled, x_t):
    step = pl.program_id(0)
    tile = core_ref.shape[1]
    rank = x_ref.shape[1]
    chunk = min(512, rank)
    amp = amp_ref[...]

    @pl.when(step == 0)
    def _():
        for c in range(0, rank, min(256, rank)):
            cut = slice(c, c + min(256, rank))
            x_t[cut, :] = x_ref[:, cut].T
        virtual = jnp.dot(fock_ref[...], amp, preferred_element_type=F32)
        out_ref[...] = int_ref[...].astype(F32) + virtual

    cols = pl.ds(pl.multiple_of(step * tile, tile), tile)
    first = jnp.dot(amp, x_ref[:, cols], preferred_element_type=F32).astype(BF16)
    for p in range(0, rank, chunk):
        middle = jnp.dot(x_t[p : p + chunk, :], first, preferred_element_type=F32)
        scaled[p : p + chunk, :] = (core_ref[p : p + chunk, :].astype(F32) * middle).astype(BF16)
    second = jnp.dot(x_ref[...], scaled[...], preferred_element_type=F32).astype(BF16)
    out_ref[...] += jnp.dot(second, x_t[cols, :], preferred_element_type=F32)


def ladder(slot, amps, ints, x, core, fock):
    virt, rank = x.shape
    tile = min(512, rank)
    pair = pl.BlockSpec((None, virt, virt), lambda q, s: (s[0], 0, 0))
    return pl.pallas_call(
        ladder_kernel,
        out_shape=jax.ShapeDtypeStruct((virt, virt), F32),
        grid_spec=pltpu.PrefetchScalarGridSpec(
            num_scalar_prefetch=1,
            grid=(rank // tile,),
            in_specs=[
                pair,
                pair,
                whole(x.shape),
                pl.BlockSpec((rank, tile), lambda q, s: (0, q)),
                whole(fock.shape),
            ],
            out_specs=whole((virt, virt)),
            scratch_shapes=[pltpu.VMEM((rank, tile), BF16), pltpu.VMEM((rank, virt), BF16)],
        ),
        compiler_params=params(54, dimension_semantics=("arbitrary",)),
        cost_estimate=pl.CostEstimate(
            flops=4 * virt * rank * (rank + virt) + 2 * virt**3,
            bytes_accessed=2 * rank * rank + 4 * virt * rank,
            transcendentals=0,
        ),
        name="ladder",
    )(slot, amps, ints, x, core, fock)


def half_kernel(slot, part_a, part_b, sum_ref, send_a, send_b, low_b, high_b):
    core = slot[0]
    send_a[...] = (part_a[...] - sum_ref[core].astype(F32)).astype(BF16)
    rounded = (part_b[...] - sum_ref[1 - core].astype(F32)).astype(BF16)
    send_b[...] = rounded

    @pl.when(pl.program_id(0) == 0)
    def _():
        low_b[...] = rounded

    @pl.when(pl.program_id(0) == 1)
    def _():
        high_b[...] = rounded


def half_of(slot, part_a, part_b, sums):
    virt = part_a.shape[0]
    rows = virt // 2
    strip = pl.BlockSpec((rows, virt), lambda r, s: (r, 0))
    return pl.pallas_call(
        half_kernel,
        out_shape=[jax.ShapeDtypeStruct((n, virt), BF16) for n in (virt, virt, rows, rows)],
        grid_spec=pltpu.PrefetchScalarGridSpec(
            num_scalar_prefetch=1,
            grid=(2,),
            in_specs=[strip, strip, pl.BlockSpec((2, rows, virt), lambda r, s: (0, r, 0))],
            out_specs=[strip, strip, whole((rows, virt)), whole((rows, virt))],
        ),
        compiler_params=params(16),
        cost_estimate=pl.CostEstimate(
            flops=0, bytes_accessed=16 * part_a.size, transcendentals=0
        ),
        name="half",
    )(slot, part_a, part_b, sums)


def finish_kernel(ids, part_a, part_b, sum_ref, amp_ref, col_ref, row_ref, occ_ref, *refs):
    near_a, far_a, same_a, low_b, near_b, far_b, same_b, res_ref, new_ref = refs
    step = pl.program_id(0)
    middle, diagonal = ids[5] == 1, ids[5] == 2

    def finish(part_ref, first, mirror):
        half = part_ref[...] - sum_ref[...].astype(F32)
        residual = half + mirror.T.astype(F32)
        denominator = col_ref[...] + row_ref[...] - occ_ref[first] - occ_ref[ids[4]]
        res_ref[...] = residual
        new_ref[...] = (amp_ref[...].astype(F32) - residual / denominator).astype(BF16)

    @pl.when(step < 2)
    def _():
        mirror = jnp.where(middle, far_a[...], near_a[...])
        finish(part_a, ids[1], jnp.where(diagonal, same_a[...], mirror))

    @pl.when(step >= 2)
    def _():
        high = jnp.where(middle, far_b[...], near_b[...])
        mirror = jnp.concatenate([low_b[...], high], axis=0)
        finish(part_b, ids[3], jnp.where(diagonal, same_b[...], mirror))


def finish(ids, part_a, part_b, sums, amps, eps_col, eps_row, eps_occ, mirror_a, mirror_b):
    virt = part_a.shape[0]
    rows = virt // 2
    strip = pl.BlockSpec(
        (None, rows, virt), lambda g, s: (jnp.where(g < 2, s[0], s[2]), g % 2, 0)
    )

    def early(g, s):
        return jnp.minimum(g, 1)

    def late(g, s):
        return jnp.maximum(g - 2, 0)

    def across(m, at, *kinds):
        def block(g, s):
            used = functools.reduce(jnp.logical_or, [s[5] == k for k in kinds])
            return (0, jnp.where(used, at(g, s), 0))

        return pl.BlockSpec((m.shape[0], rows), block)

    return pl.pallas_call(
        finish_kernel,
        out_shape=[
            jax.ShapeDtypeStruct(amps.shape, F32),
            jax.ShapeDtypeStruct(amps.shape, BF16),
        ],
        grid_spec=pltpu.PrefetchScalarGridSpec(
            num_scalar_prefetch=1,
            grid=(4,),
            in_specs=[
                pl.BlockSpec((rows, virt), lambda g, s: (early(g, s), 0)),
                pl.BlockSpec((rows, virt), lambda g, s: (late(g, s), 0)),
                strip,
                strip,
                pl.BlockSpec((rows, 1), lambda g, s: (g % 2, 0)),
                whole((1, virt)),
                pl.BlockSpec(memory_space=pltpu.SMEM),
            ]
            + [across(m, early, k) for m, k in zip(mirror_a, range(3))]
            + [across(mirror_b[0], late, 0, 1)]
            + [across(m, late, k) for m, k in zip(mirror_b[1:], range(3))],
            out_specs=[strip, strip],
        ),
        compiler_params=params(52, dimension_semantics=("arbitrary",)),
        cost_estimate=pl.CostEstimate(
            flops=40 * part_a.size, bytes_accessed=28 * part_a.size, transcendentals=0
        ),
        name="finish",
    )(ids, part_a, part_b, sums, amps, eps_col, eps_row, eps_occ, *mirror_a, *mirror_b)


def shards(
    amplitudes,
    exch_int,
    thc_factor,
    thc_core,
    fock_vir,
    eps_vir,
    eps_occ,
    fock_occ,
    couple_list,
    couple_count,
):
    rows_i, _, virt, _ = amplitudes.shape
    n_first = lax.axis_size("occi")
    n_second = lax.axis_size("occj")
    me_i = lax.axis_index("occi")
    me_j = lax.axis_index("occj")
    core = me_j % 2
    slot_a = jnp.reshape(core, (1,)).astype(jnp.int32)
    slot_b = 1 - slot_a
    amps = amplitudes.reshape(rows_i, virt, virt)
    ints = exch_int.reshape(rows_i, virt, virt)

    size = n_first // 2

    def spot(y, low, x, high, c):
        return (2 * y + low) * n_second + 2 * (2 * x + high) + c

    def send(array, flip, diagonal=None, middle=None, other=None):
        pairs = []
        for y in range(size):
            for x in range(size):
                apart = (x - y) % size
                route = {0: diagonal, size // 2: middle}.get(apart, other)
                for low in range(2):
                    for high in range(2):
                        for c in range(2):
                            ends = dict(
                                mirror=((y, low, x, high), (x, high, y, low)),
                                inward=((y, low, x, high), (x, low, x, high)),
                                outward=((x, low, x, high), (x, high, y, low)),
                            ).get(route)
                            if ends:
                                pairs.append((spot(*ends[0], c), spot(*ends[1], c ^ flip)))
        return lax.ppermute(array, AXES, pairs)

    apart = (me_j // 4 - me_i // 2) % size
    kind = jnp.where(apart == size // 2, 1, jnp.where(apart == 0, 2, 0))
    eps_col = eps_vir.reshape(virt, 1)
    eps_row = eps_vir.reshape(1, virt)

    pair_ids = [slot_a[0], me_i * rows_i + slot_a[0], slot_b[0], me_i * rows_i + slot_b[0]]
    ids = jnp.stack([*pair_ids, me_j, kind]).astype(jnp.int32)

    slices = amps.reshape(n_second, rows_i * virt // n_second, virt)
    slices = lax.all_to_all(slices, "occj", 0, 0, tiled=True)
    weights = coupling(fock_occ, couple_list, couple_count)
    tall = jnp.repeat(jnp.repeat(weights, SUB, axis=0), SUB, axis=1)
    lane = jnp.arange(n_second * SUB, dtype=jnp.int32) % SUB
    wide = jnp.where(lane[:, None] == lane[None, :], tall, 0.0)
    part_a = ladder(slot_a, amps, ints, thc_factor, thc_core, fock_vir)
    slices, part_a, ids, eps_col = lax.optimization_barrier((slices, part_a, ids, eps_col))
    sums = mix(wide, slices)
    sums, part_a, slot_b = lax.optimization_barrier((sums, part_a, slot_b))
    sums = lax.all_to_all(sums, "occj", 0, 0, tiled=True)
    part_b = ladder(slot_b, amps, ints, thc_factor, thc_core, fock_vir)
    sums, part_b = lax.optimization_barrier((sums, part_b))
    sums = sums.reshape(rows_i, virt, virt)
    send_a, send_b, low_b, high_b = half_of(slot_a, part_a, part_b, sums)
    near_a = send(send_a, 0, middle="inward", other="mirror")
    low_b = send(low_b, 1, middle="mirror", other="mirror")
    near_b = send(high_b, 1, middle="inward", other="mirror")
    same_a = send(send_a, 0, diagonal="mirror")
    same_b = send(send_b, 1, diagonal="mirror")
    low_b, near_b = lax.optimization_barrier((low_b, near_b))
    far_a = send(near_a, 0, middle="outward")
    far_b = send(near_b, 0, middle="outward")
    mirror_a, mirror_b = (near_a, far_a, same_a), (low_b, near_b, far_b, same_b)
    residual, updated = finish(
        ids, part_a, part_b, sums, amps, eps_col, eps_row, eps_occ, mirror_a, mirror_b
    )
    return (
        residual.reshape(rows_i, 1, virt, virt),
        updated.reshape(rows_i, 1, virt, virt),
    )


def solution(mesh):
    pairs = P("occi", "occj", None, None)
    return jax.shard_map(
        shards,
        mesh=mesh,
        in_specs=(pairs, pairs) + (P(),) * 8,
        out_specs=(pairs, pairs),
        check_vma=False,
    )
```

```python
import functools

import jax
import jax.numpy as jnp
from jax import lax
from jax.experimental import pallas as pl
from jax.experimental.pallas import tpu as pltpu
from jax.sharding import PartitionSpec as P

AXES = ("occi", "occj")
F32 = jnp.float32
BF16 = jnp.bfloat16
SUB = 16


def coupling(fock_occ, couple_list, couple_count):
    n_occ = fock_occ.shape[0]
    slots = jnp.arange(couple_list.shape[1], dtype=jnp.int32)
    active = slots[None, :] < couple_count[:, None]
    target = jnp.arange(n_occ, dtype=jnp.int32)
    hits = (couple_list[:, :, None] == target[None, None, :]) & active[:, :, None]
    return fock_occ * jnp.sum(hits.astype(fock_occ.dtype), axis=1)


def params(limit, **kw):
    return pltpu.CompilerParams(vmem_limit_bytes=limit << 20, **kw)


def whole(shape):
    return pl.BlockSpec(shape, lambda *_: (0,) * len(shape))


def mix_kernel(w_ref, in_ref, out_ref):
    n = in_ref.shape[0]
    w = w_ref[...]
    high = w.astype(BF16)
    rest = w - high.astype(F32)
    mid = rest.astype(BF16)
    low = (rest - mid.astype(F32)).astype(BF16)
    for r in range(0, in_ref.shape[1], SUB):
        rhs = jnp.concatenate([in_ref[k, r : r + SUB, :] for k in range(n)], axis=0)
        total = jnp.dot(high, rhs, preferred_element_type=F32)
        total += jnp.dot(mid, rhs, preferred_element_type=F32)
        total += jnp.dot(low, rhs, preferred_element_type=F32)
        for j in range(n):
            out_ref[j, r : r + SUB, :] = total[j * SUB : (j + 1) * SUB, :].astype(BF16)


def mix(wide, slices):
    return pl.pallas_call(
        mix_kernel,
        out_shape=jax.ShapeDtypeStruct(slices.shape, BF16),
        grid=(1,),
        in_specs=[whole(wide.shape), whole(slices.shape)],
        out_specs=whole(slices.shape),
        compiler_params=params(16),
        cost_estimate=pl.CostEstimate(
            flops=10**9, bytes_accessed=4 * slices.size, transcendentals=0
        ),
        name="mix",
    )(wide, slices)


def ladder_kernel(slot, amp_ref, int_ref, x_ref, core_ref, fock_ref, out_ref, scaled, x_t):
    step = pl.program_id(0)
    tile = core_ref.shape[1]
    rank = x_ref.shape[1]
    chunk = min(512, rank)
    amp = amp_ref[...]

    @pl.when(step == 0)
    def _():
        for c in range(0, rank, min(256, rank)):
            cut = slice(c, c + min(256, rank))
            x_t[cut, :] = x_ref[:, cut].T
        virtual = jnp.dot(fock_ref[...], amp, preferred_element_type=F32)
        out_ref[...] = int_ref[...].astype(F32) + virtual

    cols = pl.ds(pl.multiple_of(step * tile, tile), tile)
    first = jnp.dot(amp, x_ref[:, cols], preferred_element_type=F32).astype(BF16)
    for p in range(0, rank, chunk):
        middle = jnp.dot(x_t[p : p + chunk, :], first, preferred_element_type=F32)
        scaled[p : p + chunk, :] = (core_ref[p : p + chunk, :].astype(F32) * middle).astype(BF16)
    second = jnp.dot(x_ref[...], scaled[...], preferred_element_type=F32).astype(BF16)
    out_ref[...] += jnp.dot(second, x_t[cols, :], preferred_element_type=F32)


def ladder(slot, amps, ints, x, core, fock):
    virt, rank = x.shape
    tile = min(512, rank)
    pair = pl.BlockSpec((None, virt, virt), lambda q, s: (s[0], 0, 0))
    return pl.pallas_call(
        ladder_kernel,
        out_shape=jax.ShapeDtypeStruct((virt, virt), F32),
        grid_spec=pltpu.PrefetchScalarGridSpec(
            num_scalar_prefetch=1,
            grid=(rank // tile,),
            in_specs=[
                pair,
                pair,
                whole(x.shape),
                pl.BlockSpec((rank, tile), lambda q, s: (0, q)),
                whole(fock.shape),
            ],
            out_specs=whole((virt, virt)),
            scratch_shapes=[pltpu.VMEM((rank, tile), BF16), pltpu.VMEM((rank, virt), BF16)],
        ),
        compiler_params=params(54, dimension_semantics=("arbitrary",)),
        cost_estimate=pl.CostEstimate(
            flops=4 * virt * rank * (rank + virt) + 2 * virt**3,
            bytes_accessed=2 * rank * rank + 4 * virt * rank,
            transcendentals=0,
        ),
        name="ladder",
    )(slot, amps, ints, x, core, fock)


def half_kernel(slot, part_a, part_b, sum_ref, send_a, send_b, low_b, high_b):
    core = slot[0]
    send_a[...] = (part_a[...] - sum_ref[core].astype(F32)).astype(BF16)
    rounded = (part_b[...] - sum_ref[1 - core].astype(F32)).astype(BF16)
    send_b[...] = rounded

    @pl.when(pl.program_id(0) == 0)
    def _():
        low_b[...] = rounded

    @pl.when(pl.program_id(0) == 1)
    def _():
        high_b[...] = rounded


def half_of(slot, part_a, part_b, sums):
    virt = part_a.shape[0]
    rows = virt // 2
    strip = pl.BlockSpec((rows, virt), lambda r, s: (r, 0))
    return pl.pallas_call(
        half_kernel,
        out_shape=[jax.ShapeDtypeStruct((n, virt), BF16) for n in (virt, virt, rows, rows)],
        grid_spec=pltpu.PrefetchScalarGridSpec(
            num_scalar_prefetch=1,
            grid=(2,),
            in_specs=[strip, strip, pl.BlockSpec((2, rows, virt), lambda r, s: (0, r, 0))],
            out_specs=[strip, strip, whole((rows, virt)), whole((rows, virt))],
        ),
        compiler_params=params(52),
        cost_estimate=pl.CostEstimate(
            flops=0, bytes_accessed=16 * part_a.size, transcendentals=0
        ),
        name="half",
    )(slot, part_a, part_b, sums)


def finish_kernel(ids, part_a, part_b, sum_ref, amp_ref, col_ref, row_ref, occ_ref, *refs):
    near_a, far_a, same_a, low_b, near_b, far_b, same_b, res_ref, new_ref = refs
    step = pl.program_id(0)
    middle, diagonal = ids[5] == 1, ids[5] == 2

    def finish(part_ref, first, mirror):
        half = part_ref[...] - sum_ref[...].astype(F32)
        residual = half + mirror.T.astype(F32)
        denominator = col_ref[...] + row_ref[...] - occ_ref[first] - occ_ref[ids[4]]
        res_ref[...] = residual
        new_ref[...] = (amp_ref[...].astype(F32) - residual / denominator).astype(BF16)

    @pl.when(step < 2)
    def _():
        mirror = jnp.where(middle, far_a[...], near_a[...])
        finish(part_a, ids[1], jnp.where(diagonal, same_a[...], mirror))

    @pl.when(step >= 2)
    def _():
        high = jnp.where(middle, far_b[...], near_b[...])
        mirror = jnp.concatenate([low_b[...], high], axis=0)
        finish(part_b, ids[3], jnp.where(diagonal, same_b[...], mirror))


def finish(ids, part_a, part_b, sums, amps, eps_col, eps_row, eps_occ, mirror_a, mirror_b):
    virt = part_a.shape[0]
    rows = virt // 2
    strip = pl.BlockSpec(
        (None, rows, virt), lambda g, s: (jnp.where(g < 2, s[0], s[2]), g % 2, 0)
    )

    def early(g, s):
        return jnp.minimum(g, 1)

    def late(g, s):
        return jnp.maximum(g - 2, 0)

    def across(m, at, *kinds):
        def block(g, s):
            used = functools.reduce(jnp.logical_or, [s[5] == k for k in kinds])
            return (0, jnp.where(used, at(g, s), 0))

        return pl.BlockSpec((m.shape[0], rows), block)

    return pl.pallas_call(
        finish_kernel,
        out_shape=[
            jax.ShapeDtypeStruct(amps.shape, F32),
            jax.ShapeDtypeStruct(amps.shape, BF16),
        ],
        grid_spec=pltpu.PrefetchScalarGridSpec(
            num_scalar_prefetch=1,
            grid=(4,),
            in_specs=[
                pl.BlockSpec((rows, virt), lambda g, s: (early(g, s), 0)),
                pl.BlockSpec((rows, virt), lambda g, s: (late(g, s), 0)),
                strip,
                strip,
                pl.BlockSpec((rows, 1), lambda g, s: (g % 2, 0)),
                whole((1, virt)),
                pl.BlockSpec(memory_space=pltpu.SMEM),
            ]
            + [across(m, early, k) for m, k in zip(mirror_a, range(3))]
            + [across(mirror_b[0], late, 0, 1)]
            + [across(m, late, k) for m, k in zip(mirror_b[1:], range(3))],
            out_specs=[strip, strip],
        ),
        compiler_params=params(52, dimension_semantics=("arbitrary",)),
        cost_estimate=pl.CostEstimate(
            flops=40 * part_a.size, bytes_accessed=28 * part_a.size, transcendentals=0
        ),
        name="finish",
    )(ids, part_a, part_b, sums, amps, eps_col, eps_row, eps_occ, *mirror_a, *mirror_b)


def shards(
    amplitudes,
    exch_int,
    thc_factor,
    thc_core,
    fock_vir,
    eps_vir,
    eps_occ,
    fock_occ,
    couple_list,
    couple_count,
):
    rows_i, _, virt, _ = amplitudes.shape
    n_first = lax.axis_size("occi")
    n_second = lax.axis_size("occj")
    me_i = lax.axis_index("occi")
    me_j = lax.axis_index("occj")
    core = me_j % 2
    slot_a = jnp.reshape(core, (1,)).astype(jnp.int32)
    slot_b = 1 - slot_a
    amps = amplitudes.reshape(rows_i, virt, virt)
    ints = exch_int.reshape(rows_i, virt, virt)

    size = n_first // 2

    def spot(y, low, x, high, c):
        return (2 * y + low) * n_second + 2 * (2 * x + high) + c

    def send(array, flip, diagonal=None, middle=None, other=None):
        pairs = []
        for y in range(size):
            for x in range(size):
                apart = (x - y) % size
                route = {0: diagonal, size // 2: middle}.get(apart, other)
                for low in range(2):
                    for high in range(2):
                        for c in range(2):
                            ends = dict(
                                mirror=((y, low, x, high), (x, high, y, low)),
                                inward=((y, low, x, high), (x, low, x, high)),
                                outward=((x, low, x, high), (x, high, y, low)),
                            ).get(route)
                            if ends:
                                pairs.append((spot(*ends[0], c), spot(*ends[1], c ^ flip)))
        return lax.ppermute(array, AXES, pairs)

    apart = (me_j // 4 - me_i // 2) % size
    kind = jnp.where(apart == size // 2, 1, jnp.where(apart == 0, 2, 0))
    eps_col = eps_vir.reshape(virt, 1)
    eps_row = eps_vir.reshape(1, virt)

    pair_ids = [slot_a[0], me_i * rows_i + slot_a[0], slot_b[0], me_i * rows_i + slot_b[0]]
    ids = jnp.stack([*pair_ids, me_j, kind]).astype(jnp.int32)

    slices = amps.reshape(n_second, rows_i * virt // n_second, virt)
    slices = lax.all_to_all(slices, "occj", 0, 0, tiled=True)
    weights = coupling(fock_occ, couple_list, couple_count)
    tall = jnp.repeat(jnp.repeat(weights, SUB, axis=0), SUB, axis=1)
    lane = jnp.arange(n_second * SUB, dtype=jnp.int32) % SUB
    wide = jnp.where(lane[:, None] == lane[None, :], tall, 0.0)
    part_a = ladder(slot_a, amps, ints, thc_factor, thc_core, fock_vir)
    slices, part_a, ids, eps_col = lax.optimization_barrier((slices, part_a, ids, eps_col))
    sums = mix(wide, slices)
    sums, part_a, slot_b = lax.optimization_barrier((sums, part_a, slot_b))
    sums = lax.all_to_all(sums, "occj", 0, 0, tiled=True)
    part_b = ladder(slot_b, amps, ints, thc_factor, thc_core, fock_vir)
    sums, part_b = lax.optimization_barrier((sums, part_b))
    sums = sums.reshape(rows_i, virt, virt)
    send_a, send_b, low_b, high_b = half_of(slot_a, part_a, part_b, sums)
    near_a = send(send_a, 0, middle="inward", other="mirror")
    low_b = send(low_b, 1, middle="mirror", other="mirror")
    near_b = send(high_b, 1, middle="inward", other="mirror")
    same_a = send(send_a, 0, diagonal="mirror")
    same_b = send(send_b, 1, diagonal="mirror")
    low_b, near_b = lax.optimization_barrier((low_b, near_b))
    far_a = send(near_a, 0, middle="outward")
    far_b = send(near_b, 0, middle="outward")
    mirror_a, mirror_b = (near_a, far_a, same_a), (low_b, near_b, far_b, same_b)
    residual, updated = finish(
        ids, part_a, part_b, sums, amps, eps_col, eps_row, eps_occ, mirror_a, mirror_b
    )
    return (
        residual.reshape(rows_i, 1, virt, virt),
        updated.reshape(rows_i, 1, virt, virt),
    )


def solution(mesh):
    pairs = P("occi", "occj", None, None)
    return jax.shard_map(
        shards,
        mesh=mesh,
        in_specs=(pairs, pairs) + (P(),) * 8,
        out_specs=(pairs, pairs),
        check_vma=False,
    )
```
